32 devices in a mesh: dp: 8 (over z, x), seq: 4 (over y, core).
Axes of the slice: x: 2, y: 2, z: 4, core: 2. Of those that a mesh axis runs over, the one named last changes fastest.
Arguments:
- hidden: bfloat16 [16384, 2048], P(('dp', 'seq')), may hold values from -6 to 6
- grad_out: bfloat16 [16384, 2048], P(('dp', 'seq')), may hold values from -6 to 6
- doc_lengths: int32 [8, 4], P('dp'), may hold values from 1 to 1024, 2048 in all within a row
- resets: int32 [8, 4], P('dp'), may hold values 0 or 1
- width_index: int32 [8], P('dp'), may hold values from 0 to 3
- owner_counts: int32 [32], replicated, may hold values from 24 to 40, as said below
- w_in: float32 [2560, 8512], P(('dp', 'seq')), may hold values from -0.125 to 0.125
- m_in: float32 [2560, 8512], P(('dp', 'seq')), may hold values from -0.0029296875 to 0.0029296875
- v_in: float32 [2560, 8512], P(('dp', 'seq')), may hold values from 3.872789e-08 to 1.5491156e-07
- w_out: float32 [2560, 4096], P(('dp', 'seq')), may hold values from -0.125 to 0.125
- m_out: float32 [2560, 4096], P(('dp', 'seq')), may hold values from -0.0029296875 to 0.0029296875
- v_out: float32 [2560, 4096], P(('dp', 'seq')), may hold values from 3.872789e-08 to 1.5491156e-07
- small_params: float32 [28096], replicated, may hold values from -12 to 1.5, as said below
- small_m: float32 [28096], replicated
- small_v: float32 [28096], replicated, as said below
Outputs:
- output: bfloat16 [16384, 2048], P(('dp', 'seq'))
- input_grad: float32 [16384, 2048], P(('dp', 'seq'))
- w_in_new: float32 [2560, 8512], P(('dp', 'seq'))
- m_in_new: float32 [2560, 8512], P(('dp', 'seq'))
- v_in_new: float32 [2560, 8512], P(('dp', 'seq'))
- w_out_new: float32 [2560, 4096], P(('dp', 'seq'))
- m_out_new: float32 [2560, 4096], P(('dp', 'seq'))
- v_out_new: float32 [2560, 4096], P(('dp', 'seq'))
- small_new: float32 [28096], replicated
- small_m_new: float32 [28096], replicated
- small_v_new: float32 [28096], replicated
- w_in_grad: float32 [2560, 8512], P(('dp', 'seq'))
- w_out_grad: float32 [2560, 4096], P(('dp', 'seq'))
- small_grad: float32 [28096], replicated
- norm: float32 [1], replicated
The draws below stay inside these ranges and needn't reach their ends.
Inputs may be any that keep to these rules, and one draw needn't show every extreme that they name: `doc_lengths`: each row lists the 4 documents of one sequence in order and sums to 2048. `resets`: the entry of a sequence's first document has no effect. `width_index`: a sequence of width index w uses the first 64 * (w + 1) // 4 heads. `owner_counts`: the counts sum to 1024; owners hold consecutive blocks in device order; the first block of device d lies between d * 32 and d * 32 + 40 - 1024 / 32. `small_params`: gains and skip gains are positive. `small_v`: every entry is positive.
All inputs are finite; a program needn't handle non-finite values. No bound on the sum of `resets` on one device may be relied on, other than what follows from the above.
Results may differ from the reference program's by a relative error of at most 0.0093.
Values may be sent and summed in bfloat16 or wider, within the bound.
No kernel may reach another device: no remote copies, remote signals or barrier semaphores. Data moves between devices by JAX's collectives and lax.ppermute only.
A program may use at most 400 MiB of HBM per device.

```python
import math
import jax
import jax.numpy as jnp
import numpy as np
from jax import lax

D = 2048
E = 4096
H = 64
P_SIZE = 64
N = 128
K = 4
BLK = 256
RB = 2
NDOC = 4
CW = 4352
DIN = 8512
SEQ_LEN = 2048
SEQS = 8
TOKENS = 16384
NBLK = 1024
CAP = 40
SMALL = 28096
DEVICES = 32


def draw_owner_counts(key, part):
    base = NBLK // DEVICES
    spare = CAP - base
    drift = jax.random.randint(key, (DEVICES,), 0, spare + 1).astype(jnp.int32)
    drift = drift.at[0].set(spare).at[DEVICES - 1].set(0)
    before = jnp.concatenate([jnp.zeros((1,), jnp.int32), drift[:-1]])
    return (base + drift - before).astype(jnp.int32)


def draw_small_params(key, part):
    keys = jax.random.split(key, 7)
    gain_in = jax.random.uniform(keys[0], (D,), jnp.float32, 0.5, 1.5)
    conv_weight = jnp.clip(0.5 * jax.random.normal(keys[1], (K * CW,), jnp.float32), -1.5, 1.5)
    conv_bias = jax.random.uniform(keys[2], (CW,), jnp.float32, -0.5, 0.5)
    dt_bias = jax.random.uniform(keys[3], (H,), jnp.float32, -1.0, 1.0)
    decay_log = jax.random.uniform(keys[4], (H,), jnp.float32, jnp.log(0.5 / SEQ_LEN), jnp.log(1.0 / 30.0))
    skip_gain = jax.random.uniform(keys[5], (H,), jnp.float32, 0.5, 1.5)
    gain_out = jax.random.uniform(keys[6], (E,), jnp.float32, 0.5, 1.5)
    return jnp.concatenate([gain_in, conv_weight, conv_bias, dt_bias, decay_log, skip_gain, gain_out])


def segment_scale():
    base = (D * (DIN + E)) ** (-0.5)
    return jnp.concatenate([jnp.full((D + K * CW + CW,), 4.0 * base, jnp.float32), jnp.full((3 * H,), 16.0 * base, jnp.float32), jnp.full((E,), 4.0 * base, jnp.float32)])


def draw_small_m(key, part):
    return segment_scale() * jax.random.normal(key, (SMALL,), jnp.float32)


def draw_small_v(key, part):
    scale = segment_scale()
    return scale * scale * jnp.exp(jax.random.uniform(key, (SMALL,), jnp.float32, 0.0, jnp.log(4.0)))


def place_ends(drawn, rng, low, top_value):
    extent = drawn.shape
    index_at = [jax.random.randint(jax.random.fold_in(rng, axis), (), 0, extent[axis]) for axis in range(len(extent))]
    drawn = drawn.at[tuple(index_at)].set(low)
    longest = extent.index(max(extent))
    index_at[longest] = (index_at[longest] + 1) % extent[longest]
    return drawn.at[tuple(index_at)].set(top_value)


def level_of(stream_key, extent, cuts, least, top_value):
    loudness = 1.0
    for dim, shards_of in cuts:
        draws = jax.random.uniform(jax.random.fold_in(jax.random.fold_in(stream_key, 6), dim), (shards_of,), jnp.float32, least / len(cuts), top_value / len(cuts))
        loudness = loudness * jnp.repeat(jnp.exp(draws), extent[dim] // shards_of).reshape((-1,) + (1,) * (len(extent) - 1 - dim))
    return loudness


def split_up(count, total, bound, skew):
    loads = [(1 << 20) // math.isqrt(grade ** skew) + 1 for grade in range(2, count + 1)]
    spare, holding = total - bound - (count - 1), [1] * (count - 1)
    while spare > 0:
        movable = [i for i in range(count - 1) if holding[i] < bound]
        whole, remaining = sum([loads[i] for i in movable]), spare
        for i in movable:
            addition = min(bound - holding[i], max(1, remaining * loads[i] // whole), spare)
            holding[i] = holding[i] + addition
            spare = spare - addition
    return np.array([bound] + holding)


def ragged_sizes(stream_key, amount, total, reach, lean):
    if amount == 2:
        one = jax.random.randint(stream_key, (), max(1, total - reach), min(reach, total - 1) + 1)
        return jnp.stack([one, total - one])
    sizes = jnp.asarray(split_up(amount, total, reach, lean), jnp.int32)
    pairs = (amount - 1) // 2
    donor, taker = sizes[1:1 + 2 * pairs:2], sizes[2:2 + 2 * pairs:2]
    margin = jnp.minimum(donor - 1, reach - taker)
    shifted = jax.random.randint(jax.random.fold_in(stream_key, 1), (pairs,), 0, 1 << 20) % (margin + 1)
    sizes = sizes.at[1:1 + 2 * pairs:2].set(donor - shifted).at[2:2 + 2 * pairs:2].set(taker + shifted)
    return sizes[jax.random.permutation(jax.random.fold_in(stream_key, 2), amount)]


def normal_values(own_key, extent, deviation, limit, cuts=(), kind=jnp.bfloat16):
    values = jax.random.normal(own_key, extent, jnp.float32) * deviation
    if len(cuts) > 0:
        values = level_of(own_key, extent, cuts, -0.22, 0.18) * values
    return jnp.clip(values, min=-limit, max=limit).astype(kind)


def setup_inputs(seed: int = 0) -> dict:
    key_list = jax.random.split(jax.random.key(seed), 16)
    return {
        "hidden": normal_values(key_list[0], (TOKENS, D), 1.0, 6.0, ((0, 32),)),
        "grad_out": normal_values(key_list[1], (TOKENS, D), 1.0, 6.0, ((0, 32),)),
        "doc_lengths": jax.vmap(lambda own: ragged_sizes(own, NDOC, SEQ_LEN, SEQ_LEN // 2, 0))(jax.random.split(key_list[2], SEQS)).reshape((SEQS, NDOC)).astype(jnp.int32),
        "resets": place_ends((jax.random.randint(key_list[3], (SEQS, NDOC), 0, 2) < 1).astype(jnp.int32), jax.random.fold_in(key_list[3], 1), 0, 1),
        "width_index": place_ends(jax.random.randint(key_list[4], (SEQS,), 0, 4), jax.random.fold_in(key_list[4], 1), 0, 3).astype(jnp.int32),
        "owner_counts": draw_owner_counts(jax.random.fold_in(key_list[15], 71), 0),
        "w_in": normal_values(key_list[6], (DEVICES * CAP * RB, DIN), D ** -0.5, 0.125, ((0, 32),), jnp.float32),
        "m_in": normal_values(key_list[7], (DEVICES * CAP * RB, DIN), ((D * (DIN + E)) ** -0.5), 0.0029296875, ((0, 32),), jnp.float32),
        "v_in": jnp.clip(jnp.exp(math.log(1.549115609122964e-07) - 1.3862944 * jax.random.uniform(key_list[8], (DEVICES * CAP * RB, DIN), jnp.float32) ** level_of(key_list[8], (DEVICES * CAP * RB, DIN), ((0, 32),), -0.2, 0.2)), 3.87278902280741e-08, 1.549115609122964e-07),
        "w_out": normal_values(key_list[9], (DEVICES * CAP * RB, E), (E // 2) ** -0.5, 0.125, ((0, 32),), jnp.float32),
        "m_out": normal_values(key_list[10], (DEVICES * CAP * RB, E), ((D * (DIN + E)) ** -0.5), 0.0029296875, ((0, 32),), jnp.float32),
        "v_out": jnp.clip(jnp.exp(math.log(1.549115609122964e-07) - 1.3862944 * jax.random.uniform(key_list[11], (DEVICES * CAP * RB, E), jnp.float32) ** level_of(key_list[11], (DEVICES * CAP * RB, E), ((0, 32),), -0.2, 0.2)), 3.87278902280741e-08, 1.549115609122964e-07),
        "small_params": draw_small_params(jax.random.fold_in(key_list[15], 71), 0),
        "small_m": draw_small_m(jax.random.fold_in(key_list[15], 71), 0),
        "small_v": draw_small_v(jax.random.fold_in(key_list[15], 71), 0),
    }


highest = lax.Precision.HIGHEST
norm_eps = 1e-05
adam_eps = 1e-08
weight_decay = 0.1
rate_matrix = 0.02
rate_vector = 0.15
bias_fix = 1.0 - 0.5 ** 3

@jax.custom_vjp
def low(v):
    return lax.optimization_barrier(v.astype(jnp.bfloat16)).astype(jnp.float32)

@jax.custom_vjp
def low_back(v):
    return v

def low_keep(v):
    return (low(v), None)

def low_pass(kept, grad):
    return (grad,)

def back_keep(v):
    return (v, None)

def back_low(kept, grad):
    return (low(grad),)
low.defvjp(low_keep, low_pass)
low_back.defvjp(back_keep, back_low)

def unpack(small):
    offset = 0
    pieces = []
    for length in (D, K * CW, CW, H, H, H, E):
        pieces.append(lax.slice_in_dim(small, offset, offset + length))
        offset = offset + length
    return (pieces[0], pieces[1].reshape(K, CW), pieces[2], pieces[3], pieces[4], pieces[5], pieces[6])

def block_state(inputs, keys, steps, logs, resets):
    totals = jnp.cumsum(logs, axis=0)
    segment = jnp.cumsum(resets)
    last_same = (segment == segment[-1]).astype(jnp.float32)
    tail = jnp.exp(totals[-1][None, :] - totals) * last_same[:, None] * steps
    fresh = jnp.einsum('sh,shp,sn->hpn', tail, inputs, keys, precision=highest)
    carry_on = jnp.exp(totals[-1]) * (segment[-1] == 0).astype(jnp.float32)
    return (carry_on, fresh)

def block_output(inputs, keys, queries, steps, logs, resets, state_in):
    length = inputs.shape[0]
    totals = jnp.cumsum(logs, axis=0)
    segment = jnp.cumsum(resets)
    order = jnp.arange(length)
    allowed = ((segment[:, None] == segment[None, :]) & (order[:, None] >= order[None, :]))[:, :, None]
    spread = totals[:, None, :] - totals[None, :, :]
    decay = jnp.where(allowed, jnp.exp(jnp.where(allowed, spread, 0.0)), 0.0)
    scores = jnp.dot(queries, keys.T, precision=highest)
    mixing = scores[:, :, None] * decay * steps[None, :, :]
    result = jnp.einsum('tsh,shp->thp', mixing, inputs, precision=highest)
    enter = jnp.exp(totals) * (segment == 0).astype(jnp.float32)[:, None]
    return result + enter[:, :, None] * jnp.einsum('hpn,tn->thp', state_in, queries, precision=highest)

def split_blocks(array, count):
    return array.reshape((count, array.shape[0] // count) + array.shape[1:])

def local_outputs(inputs, keys, queries, steps, logs, resets, state_in):
    count = inputs.shape[0] // BLK

    def advance(state, block):
        block_inputs, block_keys, block_queries, block_steps, block_logs, block_resets = block
        result = block_output(block_inputs, block_keys, block_queries, block_steps, block_logs, block_resets, state)
        carry_on, fresh = block_state(block_inputs, block_keys, block_steps, block_logs, block_resets)
        return (carry_on[:, None, None] * state + fresh, result)
    blocks = tuple((split_blocks(array, count) for array in (inputs, keys, queries, steps, logs, resets)))
    final, results = lax.scan(jax.checkpoint(advance), state_in, blocks)
    return results.reshape(inputs.shape)

def reset_flags(lengths_row, flags_row, positions):
    starts = jnp.cumsum(lengths_row) - lengths_row
    later = jnp.arange(lengths_row.shape[0]) >= 1
    hits = (positions[:, None] == starts[None, :]) & (flags_row[None, :] == 1) & later[None, :]
    return jnp.any(hits, axis=1).astype(jnp.float32)

def width_mask(width):
    heads_on = H * (width + 1) // 4
    channel_mask = (jnp.arange(E) // P_SIZE < heads_on).astype(jnp.float32)
    return (channel_mask, (heads_on * P_SIZE).astype(jnp.float32))

def owner_tables(counts, slot):
    devices = counts.shape[0]
    ends = jnp.cumsum(counts)
    offsets = ends - counts
    within = jnp.arange(slot)
    source = offsets[:, None] * RB + within[None, :]
    alive = within[None, :] < counts[:, None] * RB
    source = jnp.where(alive, source, 0).astype(jnp.int32)
    rows = jnp.arange(D)
    blocks = rows // RB
    owner = lax.optimization_barrier(jnp.sum((ends[None, :] <= blocks[:, None]).astype(jnp.int32), axis=1))
    match = jnp.arange(devices)[None, :] == owner[:, None]
    first_row = lax.optimization_barrier(jnp.sum(jnp.where(match, offsets[None, :] * RB, 0), axis=1))
    place = (owner * slot + rows - first_row).astype(jnp.int32)
    return (source, alive, place)

def adamw(weight, first, second, grad, rate, correction):
    first_new = 0.5 * first + 0.5 * grad
    second_new = 0.5 * second + 0.5 * grad * grad
    update = first_new / correction / (jnp.sqrt(second_new / correction) + adam_eps)
    return (weight - rate * (update + weight_decay * weight), first_new, second_new)

def sequence_forward(seq_hidden, seq_flags, seq_mask, seq_active, in_low, out_low, small):
    gain_in, conv_weight, conv_bias, dt_bias, decay_log, skip_gain, gain_out = unpack(small)
    length = seq_hidden.shape[0]
    scale = lax.rsqrt(lax.optimization_barrier(jnp.mean(seq_hidden * seq_hidden, axis=1, keepdims=True)) + norm_eps)
    normed = low(seq_hidden * scale * gain_in[None, :])
    projected = low(low_back(jnp.dot(normed, in_low, precision=highest)))
    gate_raw = projected[:, :E]
    conv_in = projected[:, E:E + CW]
    dt_raw = projected[:, E + CW:]
    padded = jnp.concatenate([jnp.zeros((K - 1, CW), jnp.float32), conv_in], axis=0)
    mixed = conv_bias[None, :] + sum((conv_weight[tap][None, :] * padded[tap:tap + length] for tap in range(K)))
    activated = low(jax.nn.silu(mixed))
    steps = jax.nn.softplus(dt_raw + dt_bias[None, :])
    logs = -jnp.exp(decay_log)[None, :] * steps
    inputs = activated[:, :E] * seq_mask[None, :]
    keys = activated[:, E:E + N]
    queries = activated[:, E + N:]
    heads_in = inputs.reshape(length, H, P_SIZE)
    result = local_outputs(heads_in, keys, queries, steps, logs, seq_flags, jnp.zeros((H, P_SIZE, N), jnp.float32))
    result = result + skip_gain[None, :, None] * heads_in
    gated = result.reshape(length, E) * jax.nn.silu(gate_raw) * seq_mask[None, :]
    square = lax.optimization_barrier(jnp.sum(gated * gated, axis=1, keepdims=True)) / seq_active
    mixed_out = low(gated * lax.rsqrt(square + norm_eps) * gain_out[None, :])
    return seq_hidden + jnp.dot(mixed_out, out_low.T, precision=highest)

def reference(hidden, grad_out, doc_lengths, resets, width_index, owner_counts, w_in, m_in, v_in, w_out, m_out, v_out, small_params, small_m, small_v):
    slot = CAP * RB
    source, alive, place = owner_tables(owner_counts, slot)
    source_flat = source.reshape(-1)
    alive_flat = alive.reshape(-1)
    positions = jnp.arange(SEQ_LEN)
    flags = jax.vmap(reset_flags, in_axes=(0, 0, None))(doc_lengths, resets, positions)
    masks, actives = jax.vmap(width_mask)(width_index)
    in_natural = jnp.take(w_in, place, axis=0)
    out_natural = jnp.take(w_out, place, axis=0)

    def forward(hidden_full, in_weights, out_weights, small):
        in_low = low(in_weights)
        out_low = low(out_weights)

        def one_sequence(item):
            return sequence_forward(item[0], item[1], item[2], item[3], in_low, out_low, small)
        items = (hidden_full.reshape(SEQS, SEQ_LEN, D), flags, masks, actives)
        return lax.map(jax.checkpoint(one_sequence), items).reshape(TOKENS, D)
    result, pull = jax.vjp(forward, hidden.astype(jnp.float32), in_natural, out_natural, small_params)
    input_grad, grad_in_natural, grad_out_natural, small_grad = pull(grad_out.astype(jnp.float32))
    grad_in = jnp.where(alive_flat[:, None], jnp.take(grad_in_natural, source_flat, axis=0), 0.0)
    grad_outw = jnp.where(alive_flat[:, None], jnp.take(grad_out_natural, source_flat, axis=0), 0.0)
    norm = jnp.sqrt(jnp.sum(grad_in * grad_in) + jnp.sum(grad_outw * grad_outw) + jnp.sum(small_grad * small_grad))
    clip = 1.0 / jnp.maximum(norm, 1.0)
    correction = jnp.float32(bias_fix)
    w_in_new, m_in_new, v_in_new = adamw(w_in, m_in, v_in, grad_in * clip, rate_matrix, correction)
    w_out_new, m_out_new, v_out_new = adamw(w_out, m_out, v_out, grad_outw * clip, rate_matrix, correction)
    small_new, small_m_new, small_v_new = adamw(small_params, small_m, small_v, small_grad * clip, rate_vector, correction)
    return (result.astype(jnp.bfloat16), input_grad, w_in_new, m_in_new, v_in_new, w_out_new, m_out_new, v_out_new, small_new, small_m_new, small_v_new, grad_in, grad_outw, small_grad, norm.reshape(1))
```

```python
import jax
import jax.numpy as jnp
from jax import lax
from jax.experimental import pallas as pl
from jax.experimental.pallas import tpu as pltpu
from jax.sharding import PartitionSpec as P

D = 2048
E = 4096
H = 64
P_SIZE = 64
N = 128
K = 4
RB = 2
CW = 4352
PAIRS = E // 128

f32 = jnp.float32
bf16 = jnp.bfloat16
norm_eps = 1e-05
adam_eps = 1e-08
weight_decay = 0.1
rate_matrix = 0.02
rate_vector = 0.15
bias_fix = 1.0 - 0.5**3
OWNERS = ("dp", "seq")


def unpack(small):
    offset = 0
    pieces = []
    for length in (D, K * CW, CW, H, H, H, E):
        pieces.append(lax.slice_in_dim(small, offset, offset + length))
        offset = offset + length
    pieces[1] = pieces[1].reshape(K, CW)
    return pieces


def reset_flags(lengths_row, flags_row, positions):
    starts = jnp.cumsum(lengths_row) - lengths_row
    later = jnp.arange(lengths_row.shape[0]) >= 1
    hits = (positions[:, None] == starts[None, :]) & (flags_row[None, :] == 1) & later[None, :]
    return jnp.any(hits, axis=1).astype(f32)


def width_mask(width):
    heads_on = H * (width + 1) // 4
    channel_mask = (jnp.arange(E) // P_SIZE < heads_on).astype(f32)
    return (channel_mask, (heads_on * P_SIZE).astype(f32))


def adamw(weight, first, second, grad, rate, correction):
    first_new = 0.5 * first + 0.5 * grad
    second_new = 0.5 * second + 0.5 * grad * grad
    update = first_new / correction / (jnp.sqrt(second_new / correction) + adam_eps)
    return (weight - rate * (update + weight_decay * weight), first_new, second_new)


def even_rows(weights, count, lead, base):
    halo = weights.shape[0] - base
    devices = lax.axis_size("dp") * lax.axis_size("seq")
    last = lax.dynamic_slice_in_dim(weights, count - halo, halo, 0).astype(bf16)
    before = lax.ppermute(last, OWNERS, [(i, i + 1) for i in range(devices - 1)])
    joined = jnp.concatenate([before.astype(f32), weights], axis=0)
    return lax.dynamic_slice_in_dim(joined, halo - lead, base, 0).astype(bf16)


def owned_rows(block, count, lead, slot):
    halo = slot - block.shape[0]
    devices = lax.axis_size("dp") * lax.axis_size("seq")
    after = lax.ppermute(block[:halo], OWNERS, [(i + 1, i) for i in range(devices - 1)])
    joined = jnp.concatenate([block, after, jnp.zeros_like(after)], axis=0).astype(f32)
    picked = lax.dynamic_slice_in_dim(joined, lead, slot, 0)
    return jnp.where(jnp.arange(slot)[:, None] < count, picked, 0.0)


def exchange(value, bit, devices):
    return lax.ppermute(value, OWNERS, [(i, i ^ (1 << bit)) for i in range(devices)])


def sum_all(value, devices):
    for bit in range(devices.bit_length() - 1):
        value = value + exchange(value, bit, devices)
    return value


def split_rows(left, mine, base):
    order = jnp.arange(D)
    within = order % (D // 2)
    lowest = jnp.where(order < D // 2, 1 - mine % 2, mine % 2)
    source = (2 * (within // base) + lowest) * base + within % base
    pick = (jnp.arange(D)[:, None] == source[None, :]).astype(bf16)
    return jnp.dot(left, pick, preferred_element_type=f32).astype(bf16)


def orders_of(devices, gather):
    rest = list(range(3, devices.bit_length() - 1))
    orders = [[1, 2] + rest, [2, 1] + rest, rest[:2] + [1, 2] + rest[2:]]
    return [order[::-1] for order in orders] if gather else orders


class Reduce:
    def __init__(self, left, right, mine, base, devices, cuts):
        bits = devices.bit_length() - 1
        self.mine, self.devices, self.step = mine, devices, 0
        self.orders = orders_of(devices, False)
        self.axes = [list(range(bits - 1, 0, -1)) for _ in self.orders]
        pieces = [right[:, begin:end] for begin, end in zip((0,) + cuts, cuts + (right.shape[1],))]

        def product(features, piece):
            return lax.dot_general(features, piece, (((0,), (0,)), ((), ())), preferred_element_type=f32)

        sent = [exchange(product(left[:, : D // 2], piece).astype(bf16), 0, devices) for piece in pieces]
        self.values = [
            (product(left[:, D // 2 :], piece) + got.astype(f32))
            .astype(bf16)
            .reshape([2] * (bits - 1) + [base, piece.shape[1]])
            for piece, got in zip(pieces, sent)
        ]

    def advance(self):
        for piece, (order, axes) in enumerate(zip(self.orders, self.axes)):
            bit, value = order[self.step], self.values[piece]
            axis, own = axes.index(bit), (self.mine >> bit) & 1
            sent = lax.dynamic_index_in_dim(value, 1 - own, axis, keepdims=False).astype(bf16)
            kept = lax.dynamic_index_in_dim(value, own, axis, keepdims=False).astype(f32)
            value = kept + exchange(sent, bit, self.devices).astype(f32)
            self.values[piece] = value.astype(bf16) if self.step == 0 else value
            axes.remove(bit)
        self.step += 1

    def result(self):
        while self.step < len(self.orders[0]):
            self.advance()
        return jnp.concatenate(self.values, axis=1)


class Gather:
    def __init__(self, block, mine, devices, cuts):
        base, columns = block.shape
        half = columns // 2
        low = mine % 2
        other = lax.dynamic_slice_in_dim(block, (1 - low) * half, half, 1)
        own = lax.dynamic_slice_in_dim(block, low * half, half, 1)
        got = exchange(other, 0, devices)
        both = jnp.concatenate([jnp.where(low == 0, own, got), jnp.where(low == 0, got, own)], axis=0)
        self.mine, self.devices, self.step = mine, devices, 0
        self.orders = orders_of(devices, True)
        self.bits = [[] for _ in self.orders]
        self.values = [both[:, begin:end] for begin, end in zip((0,) + cuts, cuts + (half,))]

    def advance(self):
        for piece, (order, bits) in enumerate(zip(self.orders, self.bits)):
            bit, value = order[self.step], self.values[piece]
            own = (self.mine >> bit) & 1
            got = exchange(value, bit, self.devices)
            bits.append(bit)
            bits.sort(reverse=True)
            axis = bits.index(bit)
            self.values[piece] = jnp.stack(
                [jnp.where(own == 0, value, got), jnp.where(own == 0, got, value)], axis=axis
            )
        self.step += 1

    def result(self):
        while self.step < len(self.orders[0]):
            self.advance()
        return jnp.concatenate([value.reshape(D, value.shape[-1]) for value in self.values], axis=1)


def tie(value, *works):
    value, states = lax.optimization_barrier((value, [work.values for work in works]))
    for work, state in zip(works, states):
        work.values = state
    return value


def dot(a, b):
    return lax.dot_general(a, b, (((1,), (0,)), ((), ())), preferred_element_type=f32)


def dot_t(a, b):
    return lax.dot_general(a, b, (((1,), (1,)), ((), ())), preferred_element_type=f32)


def first_head(shape):
    return lax.broadcasted_iota(jnp.int32, shape, 1) < P_SIZE


def spread(columns, kind, left):
    return jnp.where(left, columns[:, kind : kind + 1], columns[:, 4 + kind : 5 + kind])


def note_heads(ref, value, first, left):
    lane = lax.broadcasted_iota(jnp.int32, ref.shape, 1) - first - 2 * pl.program_id(0)
    low = jnp.sum(jnp.where(left, value, 0.0), axis=1, keepdims=True)
    high = jnp.sum(jnp.where(left, 0.0, value), axis=1, keepdims=True)
    ref[...] += jnp.where(lane == 0, low, jnp.where(lane == 1, high, 0.0))


def sigmoid(v):
    return 1.0 / (1.0 + jnp.exp(-v))


def forward_kernel(
    x_ref, z_ref, cols_ref, rows_ref, g_ref, q_ref, state_ref, mask_ref, skip_ref, y_ref, gy_ref, ss_ref
):
    length = x_ref.shape[0]
    step = min(256, length)
    left = first_head(x_ref.shape)
    cols = cols_ref[0]
    x = x_ref[...].astype(f32) * mask_ref[...]
    xb = x.astype(bf16)
    inter = dot(q_ref[...], state_ref[...].astype(bf16)) * spread(cols, 3, left)
    parts = []
    for t in range(0, length, step):
        width = t + step
        outs = []
        for h in range(2):
            fall = jnp.minimum(cols[t:width, 4 * h : 4 * h + 1] - rows_ref[0, 2 * h : 2 * h + 1, :width], 0.0)
            mixing = g_ref[t:width, :width] * jnp.exp(fall) * rows_ref[0, 2 * h + 1 : 2 * h + 2, :width]
            outs.append(dot(mixing.astype(bf16), xb[:width]))
        parts.append(jnp.where(left[t:width], outs[0], outs[1]))
    y = jnp.concatenate(parts, axis=0) + inter + skip_ref[...] * x
    z = z_ref[...].astype(f32)
    gy = y * (z * sigmoid(z)) * mask_ref[...]
    y_ref[...] = y
    gy_ref[...] = gy

    @pl.when(pl.program_id(0) == 0)
    def _():
        ss_ref[...] = jnp.zeros_like(ss_ref)

    ss_ref[...] += gy * gy


def backward_kernel(
    do_ref, other_ref, own_ref, y_ref, z_ref, x_ref, cols_ref, rows_ref, gt_ref, qt_ref, state_ref, tok_ref, mask_ref, skip_ref,
    gain_ref, dz_ref, dx_ref, ds_ref, dgt_ref, dq_ref, heads_ref, vec_ref,
):
    length = x_ref.shape[0]
    step = min(256, length)
    left = first_head(x_ref.shape)
    cols = cols_ref[0]
    mask, skip, gain = mask_ref[...], skip_ref[...], gain_ref[...]
    r, pull = tok_ref[:, 0:1], tok_ref[:, 1:2]
    x = x_ref[...].astype(f32) * mask
    y = y_ref[...]
    z = z_ref[...].astype(f32)
    sig = sigmoid(z)
    gate = z * sig * mask
    gy = y * gate
    do = jnp.where(own_ref[...] > 0.5, do_ref[...], other_ref[...])
    dgy = r * do * gain - gy * pull
    dy = dgy * gate
    dz_ref[...] = (dgy * y * mask * sig * (1.0 + z * (1.0 - sig))).astype(bf16)
    vec_ref[0:1, :] = jnp.sum(do * gy * r, axis=0, keepdims=True)
    vec_ref[1:2, :] = jnp.sum(dy * x, axis=0, keepdims=True)
    vec_ref[2:8, :] = jnp.zeros((6, 128), f32)
    dyb = dy.astype(bf16)
    entering = (dy * spread(cols, 3, left)).astype(bf16)
    stateb = state_ref[...].astype(bf16)
    ds_ref[...] = dot(qt_ref[...], entering)

    @pl.when(pl.program_id(0) == 0)
    def _():
        dgt_ref[...] = jnp.zeros_like(dgt_ref)
        dq_ref[...] = jnp.zeros_like(dq_ref)
        heads_ref[...] = jnp.zeros_like(heads_ref)

    dq_ref[...] += dot_t(entering, stateb)
    xh = [jnp.where(left, x, 0.0).astype(bf16), jnp.where(left, 0.0, x).astype(bf16)]
    parts = []
    for s in range(0, length, step):
        outs = []
        total = None
        for h in range(2):
            here = cols[s : s + step]
            decay = jnp.exp(jnp.minimum(rows_ref[0, 2 * h : 2 * h + 1, s:] - here[:, 4 * h : 4 * h + 1], 0.0))
            outs.append(dot((gt_ref[s : s + step, s:] * decay).astype(bf16), dyb[s:]))
            part = dot_t(xh[h][s : s + step], dyb[s:]) * decay * here[:, 4 * h + 1 : 4 * h + 2]
            total = part if total is None else total + part
        dgt_ref[s : s + step, s:] += total
        parts.append(jnp.where(left[s : s + step], outs[0], outs[1]))
    u = jnp.concatenate(parts, axis=0)
    dx_ref[...] = spread(cols, 1, left) * u + skip * dy
    row = dy * (y - skip * x)
    xu = x * u
    note_heads(heads_ref, row, 0, left)
    note_heads(heads_ref, xu, H, left)


def conv_back(dact, in_ref, rim_ref, taps_ref, pad_ref, dc_ref, out_ref, vec_ref, edge_ref):
    length = in_ref.shape[0]
    pad_ref[0:8, :] = rim_ref[...].astype(f32)
    pad_ref[8 : 8 + length, :] = in_ref[...].astype(f32)
    c = taps_ref[4:5, :]
    for k in range(K):
        c = c + taps_ref[k : k + 1, :] * pad_ref[5 + k : 5 + k + length, :]
    sig = sigmoid(c)
    dc = dact * sig * (1.0 + c * (1.0 - sig))
    dc_ref[0:8, :] = jnp.zeros((8, 128), f32)
    dc_ref[8 : 8 + length, :] = dc
    dc_ref[8 + length : 16 + length, :] = jnp.zeros((8, 128), f32)
    for k in range(K):
        vec_ref[k : k + 1, :] = jnp.sum(dc * pad_ref[5 + k : 5 + k + length, :], axis=0, keepdims=True)
    vec_ref[4:5, :] = jnp.sum(dc, axis=0, keepdims=True)
    vec_ref[5:8, :] = jnp.zeros((3, 128), f32)
    grad = jnp.zeros((length + 8, 128), f32)
    for k in range(K):
        grad = grad + taps_ref[k : k + 1, :] * dc_ref[3 - k : 3 - k + length + 8, :]
    out_ref[...] = grad[8:].astype(bf16)
    edge_ref[0:8, :] = grad[:8]
    edge_ref[8:16, :] = grad[length:]


def inner_kernel(
    dx_ref, x_ref, cols_ref, k_ref, later_ref, mask_ref, in_ref, rim_ref, taps_ref, out_ref, vec_ref, edge_ref,
    heads_ref, dk_ref, pad_ref, dc_ref,
):
    left = first_head(x_ref.shape)
    cols = cols_ref[0]
    mask = mask_ref[...]
    x = x_ref[...].astype(f32) * mask
    later = later_ref[...].astype(bf16)
    tail, steps = spread(cols, 2, left), spread(cols, 1, left)
    u = dot(k_ref[...], later) * tail
    xu = x * u

    @pl.when(pl.program_id(0) == 0)
    def _():
        dk_ref[...] = jnp.zeros_like(dk_ref)
        heads_ref[...] = jnp.zeros_like(heads_ref)

    note_heads(heads_ref, xu, 0, left)

    dk_ref[...] += dot_t((x * tail * steps).astype(bf16), later)
    dact = (dx_ref[...] + steps * u) * mask
    conv_back(dact, in_ref, rim_ref, taps_ref, pad_ref, dc_ref, out_ref, vec_ref, edge_ref)


def outer_kernel(dact_ref, in_ref, rim_ref, taps_ref, out_ref, vec_ref, edge_ref, pad_ref, dc_ref):
    conv_back(dact_ref[...], in_ref, rim_ref, taps_ref, pad_ref, dc_ref, out_ref, vec_ref, edge_ref)


def lanes(rows, shift=0):
    return pl.BlockSpec((rows, 128), lambda i: (0, i + shift))


def turns(rows):
    return pl.BlockSpec((rows, 128), lambda i: (0, i % (PAIRS // 2)))


def whole(rows, width):
    return pl.BlockSpec((rows, width), lambda i: (0, 0))


def planes(rows, width):
    return pl.BlockSpec((1, rows, width), lambda i: (i, 0, 0))


def run(kernel, steps, ins, outs, shapes, scratch=()):
    return pl.pallas_call(
        kernel,
        grid=(steps,),
        in_specs=ins,
        out_specs=outs,
        out_shape=[jax.ShapeDtypeStruct(*shape) for shape in shapes],
        scratch_shapes=list(scratch),
        compiler_params=pltpu.CompilerParams(vmem_limit_bytes=48 * 1024 * 1024),
    )


def hand_on(fresh, carry, backward):
    count = lax.axis_size("seq")
    entered = jnp.zeros_like(fresh)
    for i in range(count - 1):
        leaving = (fresh + carry * entered).astype(bf16)
        route = [(count - 1 - i, count - 2 - i)] if backward else [(i, i + 1)]
        entered = entered + lax.ppermute(leaving, "seq", route).astype(f32)
    return entered


def local(
    hidden,
    grad_out,
    doc_lengths,
    resets,
    width_index,
    owner_counts,
    w_in,
    m_in,
    v_in,
    w_out,
    m_out,
    v_out,
    small_params,
    small_m,
    small_v,
):
    T = hidden.shape[0]
    slot = w_in.shape[0]
    seq_count = lax.axis_size("seq")
    devices = lax.axis_size("dp") * seq_count
    base = D // devices
    mine = lax.axis_index("dp") * seq_count + lax.axis_index("seq")
    gain_in, conv_weight, conv_bias, dt_bias, decay_log, skip_gain, gain_out = unpack(small_params)
    channel_mask, active = width_mask(width_index[0])
    before = jnp.arange(devices) < mine
    lead = jnp.sum(jnp.where(before, owner_counts, 0)) * RB - mine * base
    count = owner_counts[mine] * RB

    even_in = even_rows(w_in, count, lead, base)
    even_out = even_rows(w_out, count, lead, base)
    weights_x = lax.all_gather(even_in[:, E:], OWNERS, axis=0, tiled=True)
    weights_z = lax.all_gather(even_in[:, :E], OWNERS, axis=0, tiled=True)
    gather = Gather(even_out, mine, devices, (896, 1792))
    gather.advance()
    gather.advance()
    gather.advance()
    weights_x = tie(weights_x, gather)
    gather.advance()

    hidden_full = hidden.astype(f32)
    scale = lax.rsqrt(jnp.mean(hidden_full * hidden_full, axis=1, keepdims=True) + norm_eps)
    normed = (hidden_full * scale * gain_in[None, :]).astype(bf16)
    proj_x = jnp.dot(normed, weights_x, preferred_element_type=f32).astype(bf16)
    conv_in = proj_x[:, :CW]
    raw = proj_x[:, CW:].astype(f32) + dt_bias[None, :]
    route = [(i, i + 1) for i in range(seq_count - 1)]
    rim = lax.ppermute(conv_in[T - (K - 1) :], "seq", route)
    padded = jnp.concatenate([rim, conv_in], axis=0).astype(f32)
    mixed = conv_bias[None, :] + sum(
        (conv_weight[tap][None, :] * padded[tap : tap + T] for tap in range(K))
    )
    act = (mixed * sigmoid(mixed)).astype(bf16)
    keys, queries = act[:, E : E + N], act[:, E + N :]

    positions = lax.axis_index("seq") * T + jnp.arange(T)
    flags = reset_flags(doc_lengths[0], resets[0], positions)
    steps = jax.nn.softplus(raw)
    rate = jnp.exp(decay_log)[None, :]
    order = jnp.arange(T)
    lower = (order[:, None] >= order[None, :]).astype(f32)
    sums = jnp.dot(
        lower,
        jnp.concatenate([-rate * steps, jnp.broadcast_to(flags[:, None], (T, H))], axis=1),
        precision=lax.Precision.HIGHEST,
    )
    total, segment = sums[:, :H], jnp.round(sums[:, H])
    enter = jnp.exp(total) * (segment == 0)[:, None]
    tail = jnp.exp(total[-1:] - total) * (segment == segment[-1])[:, None]
    carry = jnp.repeat(enter[-1], P_SIZE)[None, :]
    cols = jnp.stack([total, steps, tail, enter], axis=2).reshape(T, PAIRS, 8).transpose(1, 0, 2)
    rows = jnp.stack([total.T, steps.T], axis=1).reshape(PAIRS, 4, T)
    allowed = (segment[:, None] == segment[None, :]) & (order[:, None] >= order[None, :])
    scores = jnp.where(allowed, jnp.einsum("tn,sn->ts", queries, keys, preferred_element_type=f32), 0.0)
    mask_row, skip_row = channel_mask[None, :], jnp.repeat(skip_gain, P_SIZE)[None, :]
    gain_row = gain_out[None, :]

    heads_of = (jnp.arange(E)[None, :] // P_SIZE == jnp.arange(H)[:, None]).astype(bf16)
    weight = jnp.dot((tail * steps).astype(bf16), heads_of, preferred_element_type=f32)
    handed = (act[:, :E].astype(f32) * mask_row * weight).astype(bf16)
    fresh = jnp.dot(keys.T, handed, preferred_element_type=f32)
    entered = hand_on(fresh, carry, False)
    weights_z = tie(weights_z, gather)
    half_out = gather.result()
    other_out = exchange(half_out, 0, devices)
    gate_raw = jnp.dot(normed, weights_z, preferred_element_type=f32).astype(bf16)
    y, gated, squares = run(
        forward_kernel,
        PAIRS,
        [lanes(T), lanes(T), planes(T, 8), planes(4, T), whole(T, T), whole(T, N), lanes(N), lanes(1), lanes(1)],
        [lanes(T), lanes(T), whole(T, 128)],
        [((T, E), f32), ((T, E), f32), ((T, 128), f32)],
    )(act, gate_raw, cols, rows, scores, queries, entered, mask_row, skip_row)
    root = lax.rsqrt(jnp.sum(squares, axis=1, keepdims=True) / active + norm_eps)
    mixed_low = (gated * root * gain_row).astype(bf16)
    half = E // 2
    own_at, other_at = (mine % 2) * half, (1 - mine % 2) * half

    def halves(array):
        return [lax.dynamic_slice_in_dim(array, at, half, 1) for at in (own_at, other_at)]

    out = Reduce(split_rows(grad_out, mine, base), mixed_low, mine, base, devices, (1664, 3328))
    grad_own = jnp.dot(grad_out, half_out, preferred_element_type=f32)
    grad_other = jnp.dot(grad_out, other_out, preferred_element_type=f32)
    grad_own, grad_other = tie((grad_own, grad_other), out)
    out.advance()
    gain_own, gain_other = halves(gain_row)
    gated_own, gated_other = halves(gated)
    along_own = jnp.sum(grad_own * gain_own * gated_own, axis=1, keepdims=True)
    along_other = jnp.sum(grad_other * gain_other * gated_other, axis=1, keepdims=True)
    pull = root**3 * (along_own + along_other) / active
    own_row = (jnp.arange(E)[None, :] // half == mine % 2).astype(f32)
    tok = jnp.concatenate([root, pull, jnp.zeros((T, 6), f32)], axis=1)
    grad_gate, grad_x, grad_entered, grad_scores, grad_queries, heads_a, vec_a = run(
        backward_kernel,
        PAIRS,
        [
            turns(T), turns(T), lanes(1), lanes(T), lanes(T), lanes(T), planes(T, 8), planes(4, T), whole(T, T),
            whole(N, T), lanes(N),
            whole(T, 8), lanes(1), lanes(1), lanes(1),
        ],
        [lanes(T), lanes(T), lanes(N), whole(T, T), whole(T, N), whole(T, 128), lanes(8)],
        [
            ((T, E), bf16), ((T, E), f32), ((N, E), f32), ((T, T), f32), ((T, N), f32), ((T, 128), f32),
            ((8, E), f32),
        ],
    )(grad_own, grad_other, own_row, y, gate_raw, act, cols, rows, scores.T, queries.T, entered, tok, mask_row, skip_row, gain_row)
    grad_gate, grad_entered = tie((grad_gate, grad_entered), out)
    features = split_rows(normed, mine, base)
    work_z = Reduce(features, grad_gate, mine, base, devices, (1664, 3328))
    out.advance()
    du = jnp.einsum("tc,dc->td", grad_gate, weights_z, preferred_element_type=f32)
    later = hand_on(grad_entered, carry, True)
    later, du = tie((later, du), out, work_z)
    out.advance()
    work_z.advance()
    rim8 = jnp.concatenate([jnp.zeros((8 - (K - 1), CW), bf16), rim], axis=0)
    taps = jnp.concatenate([conv_weight, conv_bias[None, :], jnp.zeros((3, CW), f32)], axis=0)
    scratch = (pltpu.VMEM((T + 16, 128), f32), pltpu.VMEM((T + 16, 128), f32))
    inner, vec_b, edge_b, heads_b, grad_keys = run(
        inner_kernel,
        PAIRS,
        [lanes(T), lanes(T), planes(T, 8), whole(T, N), lanes(N), lanes(1), lanes(T), lanes(8), lanes(8)],
        [lanes(T), lanes(8), lanes(16), whole(T, 128), whole(T, N)],
        [((T, E), bf16), ((8, E), f32), ((16, E), f32), ((T, 128), f32), ((T, N), f32)],
        scratch,
    )(grad_x, act, cols, keys, later, mask_row, proj_x, rim8, taps)
    inner, grad_keys = tie((inner, grad_keys), out, work_z)
    out.advance()
    work_z.advance()
    pairs_t = jnp.where(allowed.T, grad_scores, 0.0).astype(bf16)
    grad_keys = grad_keys + jnp.dot(pairs_t, queries, preferred_element_type=f32)
    grad_queries = grad_queries + jnp.einsum("st,sn->tn", pairs_t, keys, preferred_element_type=f32)
    outer, vec_c, edge_c = run(
        outer_kernel,
        2,
        [lanes(T), lanes(T, PAIRS), lanes(8, PAIRS), lanes(8, PAIRS)],
        [lanes(T), lanes(8), lanes(16)],
        [((T, 2 * N), bf16), ((8, 2 * N), f32), ((16, 2 * N), f32)],
        scratch,
    )(jnp.concatenate([grad_keys, grad_queries], axis=1), proj_x, rim8, taps)
    edges = jnp.concatenate([edge_b, edge_c], axis=1)
    pushed = lax.ppermute(edges[8 - (K - 1) : 8], "seq", [(i + 1, i) for i in range(seq_count - 1)])
    ends = (edges[8:] + jnp.concatenate([jnp.zeros((8 - (K - 1), CW), f32), pushed], axis=0)).astype(bf16)

    along = heads_a[:, H:] + heads_b[:, :H]
    leaving = carry * entered + fresh
    crossing = jnp.sum((later * leaving).reshape(N, H, P_SIZE), axis=(0, 2))
    upper = (order[:, None] <= order[None, :]).astype(f32)
    grad_logs = crossing[None, :] + jnp.dot(
        upper, heads_a[:, :H] - steps * along, precision=lax.Precision.HIGHEST
    )
    grad_raw = (along - rate * grad_logs) * jax.nn.sigmoid(raw)
    conv_vec = jnp.concatenate([vec_b, vec_c], axis=1)
    grad_proj = jnp.concatenate([inner, outer, grad_raw.astype(bf16)], axis=1)
    grad_proj = lax.dynamic_update_slice(grad_proj, ends, (T - 8, 0))
    grad_proj = tie(grad_proj, out, work_z)
    work_x = Reduce(features, grad_proj, mine, base, devices, (1792, 3584))
    work_z.advance()

    du = du + jnp.einsum("tc,dc->td", grad_proj, weights_x, preferred_element_type=f32)
    du, last_low = tie((du, mixed_low), work_x, work_z)
    work_x.advance()
    work_z.advance()
    mixed_own, mixed_other = halves(last_low)
    branch = jnp.einsum("te,de->td", mixed_own, half_out, preferred_element_type=f32)
    branch = branch + jnp.einsum("te,de->td", mixed_other, other_out, preferred_element_type=f32)
    output = (hidden_full + branch).astype(bf16)
    dug = du * gain_in[None, :]
    inward = jnp.mean(dug * hidden_full, axis=1, keepdims=True)
    input_grad = grad_out.astype(f32) + scale * dug - hidden_full * scale**3 * inward
    small_grad = jnp.concatenate(
        [
            jnp.sum(du * hidden_full * scale, axis=0),
            conv_vec[:K].reshape(-1),
            conv_vec[K],
            jnp.sum(grad_raw, axis=0),
            -rate[0] * jnp.sum(steps * grad_logs, axis=0),
            jnp.sum(vec_a[1].reshape(H, P_SIZE), axis=1),
            vec_a[0],
        ]
    )

    output, input_grad = tie((output, input_grad), work_x, work_z)

    block_out, block_z, block_x = out.result(), work_z.result(), work_x.result()
    block_in = jnp.concatenate([block_z, block_x], axis=1)
    big_square = jnp.sum(block_in**2) + jnp.sum(block_out**2)
    packed = jnp.concatenate([small_grad, jnp.full((64,), big_square)]).reshape(-1, 128)
    packed = sum_all(packed, devices).reshape(-1)
    small_total, square_total = packed[: small_grad.shape[0]], packed[small_grad.shape[0]]
    owned_in = owned_rows(block_in, count, lead, slot)
    owned_out = owned_rows(block_out, count, lead, slot)
    norm = jnp.sqrt(square_total + jnp.sum(small_total * small_total))
    clip = 1.0 / jnp.maximum(norm, 1.0)
    correction = jnp.float32(bias_fix)
    w_in_new, m_in_new, v_in_new = adamw(w_in, m_in, v_in, owned_in * clip, rate_matrix, correction)
    w_out_new, m_out_new, v_out_new = adamw(
        w_out, m_out, v_out, owned_out * clip, rate_matrix, correction
    )
    small_new, small_m_new, small_v_new = adamw(
        small_params, small_m, small_v, small_total * clip, rate_vector, correction
    )
    return (
        output,
        input_grad,
        w_in_new,
        m_in_new,
        v_in_new,
        w_out_new,
        m_out_new,
        v_out_new,
        small_new,
        small_m_new,
        small_v_new,
        owned_in,
        owned_out,
        small_total,
        norm.reshape(1),
    )


def solution(mesh):
    tokens, row, whole_array = P(OWNERS, None), P("dp", None), P()
    in_specs = (tokens, tokens, row, row, P("dp"), whole_array) + (tokens,) * 6 + (whole_array,) * 3
    out_specs = (tokens,) * 8 + (whole_array,) * 3 + (tokens,) * 2 + (whole_array,) * 2
    return jax.shard_map(local, mesh=mesh, in_specs=in_specs, out_specs=out_specs, check_vma=False)
```

```python
from functools import partial

import jax
import jax.numpy as jnp
from jax import lax
from jax.experimental import pallas as pl
from jax.experimental.pallas import tpu as pltpu
from jax.sharding import PartitionSpec as P

D = 2048
E = 4096
H = 64
P_SIZE = 64
N = 128
K = 4
RB = 2
CW = 4352
PAIRS = E // 128

f32 = jnp.float32
bf16 = jnp.bfloat16
norm_eps = 1e-05
adam_eps = 1e-08
weight_decay = 0.1
rate_matrix = 0.02
rate_vector = 0.15
bias_fix = 1.0 - 0.5**3
OWNERS = ("dp", "seq")


def unpack(small):
    offset = 0
    pieces = []
    for length in (D, K * CW, CW, H, H, H, E):
        pieces.append(lax.slice_in_dim(small, offset, offset + length))
        offset = offset + length
    pieces[1] = pieces[1].reshape(K, CW)
    return pieces


def reset_flags(lengths_row, flags_row, positions):
    starts = jnp.cumsum(lengths_row) - lengths_row
    later = jnp.arange(lengths_row.shape[0]) >= 1
    hits = (positions[:, None] == starts[None, :]) & (flags_row[None, :] == 1) & later[None, :]
    return jnp.any(hits, axis=1).astype(f32)


def width_mask(width):
    heads_on = H * (width + 1) // 4
    channel_mask = (jnp.arange(E) // P_SIZE < heads_on).astype(f32)
    return (channel_mask, (heads_on * P_SIZE).astype(f32))


def adamw(weight, first, second, grad, rate, correction):
    first_new = 0.5 * first + 0.5 * grad
    second_new = 0.5 * second + 0.5 * grad * grad
    update = first_new / correction / (jnp.sqrt(second_new / correction) + adam_eps)
    return (weight - rate * (update + weight_decay * weight), first_new, second_new)


def even_rows(weights, count, lead, base):
    halo = weights.shape[0] - base
    devices = lax.axis_size("dp") * lax.axis_size("seq")
    last = lax.dynamic_slice_in_dim(weights, count - halo, halo, 0).astype(bf16)
    before = lax.ppermute(last, OWNERS, [(i, i + 1) for i in range(devices - 1)])
    joined = jnp.concatenate([before.astype(f32), weights], axis=0)
    return lax.dynamic_slice_in_dim(joined, halo - lead, base, 0).astype(bf16)


def owned_rows(block, count, lead, slot):
    halo = slot - block.shape[0]
    devices = lax.axis_size("dp") * lax.axis_size("seq")
    after = lax.ppermute(block[:halo], OWNERS, [(i + 1, i) for i in range(devices - 1)])
    joined = jnp.concatenate([block, after, jnp.zeros_like(after)], axis=0).astype(f32)
    picked = lax.dynamic_slice_in_dim(joined, lead, slot, 0)
    return jnp.where(jnp.arange(slot)[:, None] < count, picked, 0.0)


def exchange(value, bit, devices):
    return lax.ppermute(value, OWNERS, [(i, i ^ (1 << bit)) for i in range(devices)])


def sum_all(value, devices):
    for bit in range(devices.bit_length() - 1):
        value = value + exchange(value, bit, devices)
    return value


def split_rows(left, mine, base):
    order = jnp.arange(D)
    within = order % (D // 2)
    lowest = jnp.where(order < D // 2, 1 - mine % 2, mine % 2)
    source = (2 * (within // base) + lowest) * base + within % base
    pick = (jnp.arange(D)[:, None] == source[None, :]).astype(bf16)
    return jnp.dot(left, pick, preferred_element_type=f32).astype(bf16)


def orders_of(devices, pieces):
    rest = list(range(3, devices.bit_length() - 1))
    return [[1, 2] + rest, [2, 1] + rest, rest[:2] + [1, 2] + rest[2:]][:pieces]


class Reduce:
    def __init__(self, left, right, mine, base, devices, cuts):
        bits = devices.bit_length() - 1
        self.mine, self.devices, self.step = mine, devices, 0
        self.orders = orders_of(devices, len(cuts) + 1)
        self.axes = [list(range(bits - 1, 0, -1)) for _ in self.orders]
        pieces = [right[:, begin:end] for begin, end in zip((0,) + cuts, cuts + (right.shape[1],))]

        def product(features, piece):
            return lax.dot_general(features, piece, (((0,), (0,)), ((), ())), preferred_element_type=f32)

        sent = [exchange(product(left[:, : D // 2], piece).astype(bf16), 0, devices) for piece in pieces]
        self.values = [
            (product(left[:, D // 2 :], piece) + got.astype(f32))
            .astype(bf16)
            .reshape([2] * (bits - 1) + [base, piece.shape[1]])
            for piece, got in zip(pieces, sent)
        ]

    def advance(self):
        for piece, (order, axes) in enumerate(zip(self.orders, self.axes)):
            bit, value = order[self.step], self.values[piece]
            axis, own = axes.index(bit), (self.mine >> bit) & 1
            sent = lax.dynamic_index_in_dim(value, 1 - own, axis, keepdims=False).astype(bf16)
            kept = lax.dynamic_index_in_dim(value, own, axis, keepdims=False).astype(f32)
            value = kept + exchange(sent, bit, self.devices).astype(f32)
            self.values[piece] = value.astype(bf16) if self.step == 0 else value
            axes.remove(bit)
        self.step += 1

    def result(self):
        while self.step < len(self.orders[0]):
            self.advance()
        return jnp.concatenate(self.values, axis=1)


def tie(value, *works):
    value, states = lax.optimization_barrier((value, [work.values for work in works]))
    for work, state in zip(works, states):
        work.values = state
    return value


def dot(a, b):
    return lax.dot_general(a, b, (((1,), (0,)), ((), ())), preferred_element_type=f32)


def dot_t(a, b):
    return lax.dot_general(a, b, (((1,), (1,)), ((), ())), preferred_element_type=f32)


def first_head(shape):
    return lax.broadcasted_iota(jnp.int32, shape, 1) < P_SIZE


def spread(columns, kind, left):
    return jnp.where(left, columns[:, kind : kind + 1], columns[:, 4 + kind : 5 + kind])


def note_heads(ref, value, first, left):
    lane = lax.broadcasted_iota(jnp.int32, ref.shape, 1) - first - 2 * pl.program_id(0)
    low = jnp.sum(jnp.where(left, value, 0.0), axis=1, keepdims=True)
    high = jnp.sum(jnp.where(left, 0.0, value), axis=1, keepdims=True)
    ref[...] += jnp.where(lane == 0, low, jnp.where(lane == 1, high, 0.0))


def sigmoid(v):
    return 1.0 / (1.0 + jnp.exp(-v))


def forward_kernel(
    x_ref, z_ref, cols_ref, rows_ref, g_ref, q_ref, state_ref, mask_ref, skip_ref, y_ref, gy_ref, ss_ref
):
    length = x_ref.shape[0]
    step = min(256, length)
    left = first_head(x_ref.shape)
    cols = cols_ref[0]
    x = x_ref[...].astype(f32) * mask_ref[...]
    xb = x.astype(bf16)
    inter = dot(q_ref[...], state_ref[...].astype(bf16)) * spread(cols, 3, left)
    parts = []
    for t in range(0, length, step):
        width = t + step
        outs = []
        for h in range(2):
            fall = jnp.minimum(cols[t:width, 4 * h : 4 * h + 1] - rows_ref[0, 2 * h : 2 * h + 1, :width], 0.0)
            mixing = g_ref[t:width, :width] * jnp.exp(fall) * rows_ref[0, 2 * h + 1 : 2 * h + 2, :width]
            outs.append(dot(mixing.astype(bf16), xb[:width]))
        parts.append(jnp.where(left[t:width], outs[0], outs[1]))
    y = jnp.concatenate(parts, axis=0) + inter + skip_ref[...] * x
    z = z_ref[...].astype(f32)
    gy = y * (z * sigmoid(z)) * mask_ref[...]
    y_ref[...] = y
    gy_ref[...] = gy

    @pl.when(pl.program_id(0) == 0)
    def _():
        ss_ref[...] = jnp.zeros_like(ss_ref)

    ss_ref[...] += gy * gy


def backward_kernel(
    do_ref, y_ref, z_ref, x_ref, cols_ref, rows_ref, gt_ref, state_ref, tok_ref, mask_ref, skip_ref,
    gain_ref, dx_ref, dgt_ref, dq_ref, heads_ref, vec_ref,
):
    length = x_ref.shape[0]
    step = min(256, length)
    left = first_head(x_ref.shape)
    cols = cols_ref[0]
    mask, skip, gain = mask_ref[...], skip_ref[...], gain_ref[...]
    r, pull = tok_ref[:, 0:1], tok_ref[:, 1:2]
    x = x_ref[...].astype(f32) * mask
    y = y_ref[...]
    z = z_ref[...].astype(f32)
    sig = sigmoid(z)
    gate = z * sig * mask
    gy = y * gate
    do = do_ref[...]
    dgy = r * do * gain - gy * pull
    dy = dgy * gate
    vec_ref[0:1, :] = jnp.sum(do * gy * r, axis=0, keepdims=True)
    vec_ref[1:2, :] = jnp.sum(dy * x, axis=0, keepdims=True)
    vec_ref[2:8, :] = jnp.zeros((6, 128), f32)
    dyb = dy.astype(bf16)
    entering = (dy * spread(cols, 3, left)).astype(bf16)
    stateb = state_ref[...].astype(bf16)

    @pl.when(pl.program_id(0) == 0)
    def _():
        dgt_ref[...] = jnp.zeros_like(dgt_ref)
        dq_ref[...] = jnp.zeros_like(dq_ref)
        heads_ref[...] = jnp.zeros_like(heads_ref)

    dq_ref[...] += dot_t(entering, stateb)
    xh = [jnp.where(left, x, 0.0).astype(bf16), jnp.where(left, 0.0, x).astype(bf16)]
    parts = []
    for s in range(0, length, step):
        outs = []
        total = None
        for h in range(2):
            here = cols[s : s + step]
            decay = jnp.exp(jnp.minimum(rows_ref[0, 2 * h : 2 * h + 1, s:] - here[:, 4 * h : 4 * h + 1], 0.0))
            outs.append(dot((gt_ref[s : s + step, s:] * decay).astype(bf16), dyb[s:]))
            part = dot_t(xh[h][s : s + step], dyb[s:]) * decay * here[:, 4 * h + 1 : 4 * h + 2]
            total = part if total is None else total + part
        dgt_ref[s : s + step, s:] += total
        parts.append(jnp.where(left[s : s + step], outs[0], outs[1]))
    u = jnp.concatenate(parts, axis=0)
    dx_ref[...] = spread(cols, 1, left) * u + skip * dy
    row = dy * (y - skip * x)
    xu = x * u
    note_heads(heads_ref, row, 0, left)
    note_heads(heads_ref, xu, H, left)


def conv_back(dact, in_ref, rim_ref, taps_ref, pad_ref, dc_ref, out_ref, vec_ref, edge_ref):
    length = in_ref.shape[0]
    pad_ref[0:8, :] = rim_ref[...].astype(f32)
    pad_ref[8 : 8 + length, :] = in_ref[...].astype(f32)
    c = taps_ref[4:5, :]
    for k in range(K):
        c = c + taps_ref[k : k + 1, :] * pad_ref[5 + k : 5 + k + length, :]
    sig = sigmoid(c)
    dc = dact * sig * (1.0 + c * (1.0 - sig))
    dc_ref[0:8, :] = jnp.zeros((8, 128), f32)
    dc_ref[8 : 8 + length, :] = dc
    dc_ref[8 + length : 16 + length, :] = jnp.zeros((8, 128), f32)
    for k in range(K):
        vec_ref[k : k + 1, :] = jnp.sum(dc * pad_ref[5 + k : 5 + k + length, :], axis=0, keepdims=True)
    vec_ref[4:5, :] = jnp.sum(dc, axis=0, keepdims=True)
    vec_ref[5:8, :] = jnp.zeros((3, 128), f32)
    grad = jnp.zeros((length + 8, 128), f32)
    for k in range(K):
        grad = grad + taps_ref[k : k + 1, :] * dc_ref[3 - k : 3 - k + length + 8, :]
    out_ref[...] = grad[8:].astype(bf16)
    edge_ref[0:8, :] = grad[:8]
    edge_ref[8:16, :] = grad[length:]


def inner_kernel(
    first, dx_ref, x_ref, cols_ref, k_ref, later_ref, mask_ref, in_ref, rim_ref, taps_ref, out_ref, vec_ref, edge_ref,
    heads_ref, dk_ref, pad_ref, dc_ref,
):
    left = first_head(x_ref.shape)
    cols = cols_ref[0]
    mask = mask_ref[...]
    x = x_ref[...].astype(f32) * mask
    later = later_ref[...].astype(bf16)
    tail, steps = spread(cols, 2, left), spread(cols, 1, left)
    u = dot(k_ref[...], later) * tail
    xu = x * u

    @pl.when(pl.program_id(0) == 0)
    def _():
        dk_ref[...] = jnp.zeros_like(dk_ref)
        heads_ref[...] = jnp.zeros_like(heads_ref)

    note_heads(heads_ref, xu, first, left)

    dk_ref[...] += dot_t((x * tail * steps).astype(bf16), later)
    dact = (dx_ref[...] + steps * u) * mask
    conv_back(dact, in_ref, rim_ref, taps_ref, pad_ref, dc_ref, out_ref, vec_ref, edge_ref)


def outer_kernel(dact_ref, in_ref, rim_ref, taps_ref, out_ref, vec_ref, edge_ref, pad_ref, dc_ref):
    conv_back(dact_ref[...], in_ref, rim_ref, taps_ref, pad_ref, dc_ref, out_ref, vec_ref, edge_ref)


def lanes(rows, shift=0):
    return pl.BlockSpec((rows, 128), lambda i: (0, i + shift))


def whole(rows, width):
    return pl.BlockSpec((rows, width), lambda i: (0, 0))


def planes(rows, width, shift=0):
    return pl.BlockSpec((1, rows, width), lambda i: (i + shift, 0, 0))


def run(kernel, steps, ins, outs, shapes, scratch=()):
    return pl.pallas_call(
        kernel,
        grid=(steps,),
        in_specs=ins,
        out_specs=outs,
        out_shape=[jax.ShapeDtypeStruct(*shape) for shape in shapes],
        scratch_shapes=list(scratch),
        compiler_params=pltpu.CompilerParams(vmem_limit_bytes=48 * 1024 * 1024),
    )


def hand_on(fresh, carry, backward):
    count = lax.axis_size("seq")
    entered = jnp.zeros_like(fresh)
    for i in range(count - 1):
        leaving = (fresh + carry * entered).astype(bf16)
        route = [(count - 1 - i, count - 2 - i)] if backward else [(i, i + 1)]
        entered = entered + lax.ppermute(leaving, "seq", route).astype(f32)
    return entered


def local(
    hidden,
    grad_out,
    doc_lengths,
    resets,
    width_index,
    owner_counts,
    w_in,
    m_in,
    v_in,
    w_out,
    m_out,
    v_out,
    small_params,
    small_m,
    small_v,
):
    T = hidden.shape[0]
    slot = w_in.shape[0]
    seq_count = lax.axis_size("seq")
    devices = lax.axis_size("dp") * seq_count
    base = D // devices
    mine = lax.axis_index("dp") * seq_count + lax.axis_index("seq")
    gain_in, conv_weight, conv_bias, dt_bias, decay_log, skip_gain, gain_out = unpack(small_params)
    channel_mask, active = width_mask(width_index[0])
    before = jnp.arange(devices) < mine
    lead = jnp.sum(jnp.where(before, owner_counts, 0)) * RB - mine * base
    count = owner_counts[mine] * RB

    even_in = even_rows(w_in, count, lead, base)
    even_out = even_rows(w_out, count, lead, base)
    weights_x = lax.all_gather(even_in[:, E:], OWNERS, axis=0, tiled=True)
    weights_z = lax.all_gather(even_in[:, :E], OWNERS, axis=0, tiled=True)
    tokens_out = split_rows(grad_out, mine, base)
    weights_x, tokens_out = lax.optimization_barrier((weights_x, tokens_out))

    hidden_full = hidden.astype(f32)
    scale = lax.rsqrt(jnp.mean(hidden_full * hidden_full, axis=1, keepdims=True) + norm_eps)
    normed = (hidden_full * scale * gain_in[None, :]).astype(bf16)
    proj_x = jnp.dot(normed, weights_x, preferred_element_type=f32).astype(bf16)
    conv_in = proj_x[:, :CW]
    raw = proj_x[:, CW:].astype(f32) + dt_bias[None, :]
    route = [(i, i + 1) for i in range(seq_count - 1)]
    rim = lax.ppermute(conv_in[T - (K - 1) :], "seq", route)
    padded = jnp.concatenate([rim, conv_in], axis=0).astype(f32)
    mixed = conv_bias[None, :] + sum(
        (conv_weight[tap][None, :] * padded[tap : tap + T] for tap in range(K))
    )
    act = (mixed * sigmoid(mixed)).astype(bf16)
    keys, queries = act[:, E : E + N], act[:, E + N :]

    positions = lax.axis_index("seq") * T + jnp.arange(T)
    flags = reset_flags(doc_lengths[0], resets[0], positions)
    steps = jax.nn.softplus(raw)
    rate = jnp.exp(decay_log)[None, :]
    order = jnp.arange(T)
    lower = (order[:, None] >= order[None, :]).astype(f32)
    sums = jnp.dot(
        lower,
        jnp.concatenate([-rate * steps, jnp.broadcast_to(flags[:, None], (T, H))], axis=1),
        precision=lax.Precision.HIGHEST,
    )
    total, segment = sums[:, :H], jnp.round(sums[:, H])
    enter = jnp.exp(total) * (segment == 0)[:, None]
    tail = jnp.exp(total[-1:] - total) * (segment == segment[-1])[:, None]
    carry = jnp.repeat(enter[-1], P_SIZE)[None, :]
    cols = jnp.stack([total, steps, tail, enter], axis=2).reshape(T, PAIRS, 8).transpose(1, 0, 2)
    rows = jnp.stack([total.T, steps.T], axis=1).reshape(PAIRS, 4, T)
    allowed = (segment[:, None] == segment[None, :]) & (order[:, None] >= order[None, :])
    scores = jnp.where(allowed, jnp.einsum("tn,sn->ts", queries, keys, preferred_element_type=f32), 0.0)
    mask_row, skip_row = channel_mask[None, :], jnp.repeat(skip_gain, P_SIZE)[None, :]
    gain_row = gain_out[None, :]

    heads_of = (jnp.arange(E)[None, :] // P_SIZE == jnp.arange(H)[:, None]).astype(bf16)
    weight = jnp.dot((tail * steps).astype(bf16), heads_of, preferred_element_type=f32)
    handed = (act[:, :E].astype(f32) * mask_row * weight).astype(bf16)
    fresh = jnp.dot(keys.T, handed, preferred_element_type=f32)
    entry = jnp.dot(enter.astype(bf16), heads_of, preferred_element_type=f32).astype(bf16)
    even_out, weights_z, fresh, cols, rows, scores, entry = lax.optimization_barrier(
        (even_out, weights_z, fresh, cols, rows, scores, entry)
    )
    weights_out = lax.all_gather(even_out, OWNERS, axis=0, tiled=True)
    entered = hand_on(fresh, carry, False)
    gate_raw = jnp.dot(normed, weights_z, preferred_element_type=f32).astype(bf16)
    y, gated, squares = run(
        forward_kernel,
        PAIRS,
        [lanes(T), lanes(T), planes(T, 8), planes(4, T), whole(T, T), whole(T, N), lanes(N), lanes(1), lanes(1)],
        [lanes(T), lanes(T), whole(T, 128)],
        [((T, E), f32), ((T, E), f32), ((T, 128), f32)],
    )(act, gate_raw, cols, rows, scores, queries, entered, mask_row, skip_row)
    root = lax.rsqrt(jnp.sum(squares, axis=1, keepdims=True) / active + norm_eps)
    mixed_low = (gated * root * gain_row).astype(bf16)
    out = Reduce(tokens_out, mixed_low, mine, base, devices, (2048,))
    weights_out = tie(weights_out, out)
    out.advance()
    mixed_grad = jnp.dot(grad_out, weights_out, preferred_element_type=f32)
    pull = root**3 * jnp.sum(mixed_grad * gain_row * gated, axis=1, keepdims=True) / active
    gate_full = gate_raw.astype(f32)
    open_part = sigmoid(gate_full)
    grad_gated = root * mixed_grad * gain_row - gated * pull
    grad_gate = grad_gated * y * mask_row * open_part * (1.0 + gate_full * (1.0 - open_part))
    grad_gate = grad_gate.astype(bf16)
    entering = (grad_gated * (gate_full * open_part) * mask_row * entry).astype(bf16)
    grad_entered = jnp.dot(queries.T, entering, preferred_element_type=f32)
    features = split_rows(normed, mine, base)
    work_z = Reduce(features, grad_gate, mine, base, devices, (2048,))
    mixed_grad = tie(mixed_grad, out, work_z)
    out.advance()
    work_z.advance()
    tok = jnp.concatenate([root, pull, jnp.zeros((T, 6), f32)], axis=1)
    grad_x, grad_scores, grad_queries, heads_a, vec_a = run(
        backward_kernel,
        PAIRS,
        [
            lanes(T), lanes(T), lanes(T), lanes(T), planes(T, 8), planes(4, T), whole(T, T), lanes(N), whole(T, 8),
            lanes(1), lanes(1), lanes(1),
        ],
        [lanes(T), whole(T, T), whole(T, N), whole(T, 128), lanes(8)],
        [((T, E), f32), ((T, T), f32), ((T, N), f32), ((T, 128), f32), ((8, E), f32)],
    )(mixed_grad, y, gate_raw, act, cols, rows, scores.T, entered, tok, mask_row, skip_row, gain_row)
    later = hand_on(grad_entered, carry, True)
    grad_x, grad_gate = tie((grad_x, grad_gate), out, work_z)
    out.advance()
    work_z.advance()
    du = jnp.einsum("tc,dc->td", grad_gate, weights_z, preferred_element_type=f32)
    later, du = tie((later, du), out, work_z)
    out.advance()
    work_z.advance()
    rim8 = jnp.concatenate([jnp.zeros((8 - (K - 1), CW), bf16), rim], axis=0)
    taps = jnp.concatenate([conv_weight, conv_bias[None, :], jnp.zeros((3, CW), f32)], axis=0)
    scratch = (pltpu.VMEM((T + 16, 128), f32), pltpu.VMEM((T + 16, 128), f32))
    part = PAIRS // 2

    def inner_half(shift, later):
        return run(
            partial(inner_kernel, 2 * shift),
            part,
            [
                lanes(T, shift), lanes(T, shift), planes(T, 8, shift), whole(T, N), lanes(N, shift), lanes(1, shift),
                lanes(T, shift), lanes(8, shift), lanes(8, shift),
            ],
            [lanes(T), lanes(8), lanes(16), whole(T, 128), whole(T, N)],
            [((T, E // 2), bf16), ((8, E // 2), f32), ((16, E // 2), f32), ((T, 128), f32), ((T, N), f32)],
            scratch,
        )(grad_x, act, cols, keys, later, mask_row, proj_x, rim8, taps)

    def ends_of(edges):
        route = [(i + 1, i) for i in range(seq_count - 1)]
        pushed = lax.ppermute(edges[8 - (K - 1) : 8], "seq", route)
        kept = jnp.zeros((8 - (K - 1), edges.shape[1]), f32)
        return (edges[8:] + jnp.concatenate([kept, pushed], axis=0)).astype(bf16)

    inner_a, vec_a2, edge_a, heads_b, keys_a = inner_half(0, later)
    grad_proj_a = lax.dynamic_update_slice(inner_a, ends_of(edge_a), (T - 8, 0))
    work_a = Reduce(features, grad_proj_a, mine, base, devices, (1024,))
    later_b = tie(later, out, work_z, work_a)
    work_a.advance()
    inner_b, vec_b, edge_b, heads_c, grad_keys = inner_half(part, later_b)
    inner_b, grad_keys = tie((inner_b, grad_keys), work_a)
    work_z.advance()
    work_a.advance()
    grad_keys = grad_keys + keys_a
    pairs_t = jnp.where(allowed.T, grad_scores, 0.0).astype(bf16)
    grad_keys = grad_keys + jnp.dot(pairs_t, queries, preferred_element_type=f32)
    grad_queries = grad_queries + jnp.einsum("st,sn->tn", pairs_t, keys, preferred_element_type=f32)
    outer, vec_c, edge_c = run(
        outer_kernel,
        2,
        [lanes(T), lanes(T, PAIRS), lanes(8, PAIRS), lanes(8, PAIRS)],
        [lanes(T), lanes(8), lanes(16)],
        [((T, 2 * N), bf16), ((8, 2 * N), f32), ((16, 2 * N), f32)],
        scratch,
    )(jnp.concatenate([grad_keys, grad_queries], axis=1), proj_x, rim8, taps)
    ends = ends_of(jnp.concatenate([edge_b, edge_c], axis=1))

    along = heads_a[:, H:] + heads_b[:, :H] + heads_c[:, :H]
    leaving = carry * entered + fresh
    crossing = jnp.sum((later * leaving).reshape(N, H, P_SIZE), axis=(0, 2))
    upper = (order[:, None] <= order[None, :]).astype(f32)
    grad_logs = crossing[None, :] + jnp.dot(
        upper, heads_a[:, :H] - steps * along, precision=lax.Precision.HIGHEST
    )
    grad_raw = (along - rate * grad_logs) * jax.nn.sigmoid(raw)
    conv_vec = jnp.concatenate([vec_a2, vec_b, vec_c], axis=1)
    grad_proj = jnp.concatenate([inner_b, outer, grad_raw.astype(bf16)], axis=1)
    grad_proj = lax.dynamic_update_slice(grad_proj, ends, (T - 8, 0))
    grad_proj = tie(grad_proj, work_a, work_z)
    work_a.advance()
    work_x = Reduce(features, grad_proj, mine, base, devices, (1024, 2048))

    grad_last, last_low = tie((grad_proj, mixed_low), work_x, work_a)
    work_x.advance()
    work_a.advance()
    du = du + jnp.einsum("tc,dc->td", grad_proj_a, weights_x[:, : E // 2], preferred_element_type=f32)
    du = du + jnp.einsum("tc,dc->td", grad_last, weights_x[:, E // 2 :], preferred_element_type=f32)
    branch = jnp.einsum("te,de->td", last_low, weights_out, preferred_element_type=f32)
    output = (hidden_full + branch).astype(bf16)
    dug = du * gain_in[None, :]
    inward = jnp.mean(dug * hidden_full, axis=1, keepdims=True)
    input_grad = grad_out.astype(f32) + scale * dug - hidden_full * scale**3 * inward
    small_grad = jnp.concatenate(
        [
            jnp.sum(du * hidden_full * scale, axis=0),
            conv_vec[:K].reshape(-1),
            conv_vec[K],
            jnp.sum(grad_raw, axis=0),
            -rate[0] * jnp.sum(steps * grad_logs, axis=0),
            jnp.sum(vec_a[1].reshape(H, P_SIZE), axis=1),
            vec_a[0],
        ]
    )

    output, input_grad = tie((output, input_grad), work_x, work_a)

    block_out, block_z = out.result(), work_z.result()
    block_x = jnp.concatenate([work_a.result(), work_x.result()], axis=1)
    block_in = jnp.concatenate([block_z, block_x], axis=1)
    big_square = jnp.sum(block_in**2) + jnp.sum(block_out**2)
    packed = jnp.concatenate([small_grad, jnp.full((64,), big_square)]).reshape(-1, 128)
    packed = sum_all(packed, devices).reshape(-1)
    small_total, square_total = packed[: small_grad.shape[0]], packed[small_grad.shape[0]]
    owned_in = owned_rows(block_in, count, lead, slot)
    owned_out = owned_rows(block_out, count, lead, slot)
    norm = jnp.sqrt(square_total + jnp.sum(small_total * small_total))
    clip = 1.0 / jnp.maximum(norm, 1.0)
    correction = jnp.float32(bias_fix)
    w_in_new, m_in_new, v_in_new = adamw(w_in, m_in, v_in, owned_in * clip, rate_matrix, correction)
    w_out_new, m_out_new, v_out_new = adamw(
        w_out, m_out, v_out, owned_out * clip, rate_matrix, correction
    )
    small_new, small_m_new, small_v_new = adamw(
        small_params, small_m, small_v, small_total * clip, rate_vector, correction
    )
    return (
        output,
        input_grad,
        w_in_new,
        m_in_new,
        v_in_new,
        w_out_new,
        m_out_new,
        v_out_new,
        small_new,
        small_m_new,
        small_v_new,
        owned_in,
        owned_out,
        small_total,
        norm.reshape(1),
    )


def solution(mesh):
    tokens, row, whole_array = P(OWNERS, None), P("dp", None), P()
    in_specs = (tokens, tokens, row, row, P("dp"), whole_array) + (tokens,) * 6 + (whole_array,) * 3
    out_specs = (tokens,) * 8 + (whole_array,) * 3 + (tokens,) * 2 + (whole_array,) * 2
    return jax.shard_map(local, mesh=mesh, in_specs=in_specs, out_specs=out_specs, check_vma=False)
```

```python
from functools import partial

import jax
import jax.numpy as jnp
from jax import lax
from jax.experimental import pallas as pl
from jax.experimental.pallas import tpu as pltpu
from jax.sharding import PartitionSpec as P

D = 2048
E = 4096
H = 64
P_SIZE = 64
N = 128
K = 4
RB = 2
CW = 4352
PAIRS = E // 128

f32 = jnp.float32
bf16 = jnp.bfloat16
norm_eps = 1e-05
adam_eps = 1e-08
weight_decay = 0.1
rate_matrix = 0.02
rate_vector = 0.15
bias_fix = 1.0 - 0.5**3
OWNERS = ("dp", "seq")


def unpack(small):
    offset = 0
    pieces = []
    for length in (D, K * CW, CW, H, H, H, E):
        pieces.append(lax.slice_in_dim(small, offset, offset + length))
        offset = offset + length
    pieces[1] = pieces[1].reshape(K, CW)
    return pieces


def reset_flags(lengths_row, flags_row, positions):
    starts = jnp.cumsum(lengths_row) - lengths_row
    later = jnp.arange(lengths_row.shape[0]) >= 1
    hits = (positions[:, None] == starts[None, :]) & (flags_row[None, :] == 1) & later[None, :]
    return jnp.any(hits, axis=1).astype(f32)


def width_mask(width):
    heads_on = H * (width + 1) // 4
    channel_mask = (jnp.arange(E) // P_SIZE < heads_on).astype(f32)
    return (channel_mask, (heads_on * P_SIZE).astype(f32))


def adamw(weight, first, second, grad, rate, correction):
    first_new = 0.5 * first + 0.5 * grad
    second_new = 0.5 * second + 0.5 * grad * grad
    update = first_new / correction / (jnp.sqrt(second_new / correction) + adam_eps)
    return (weight - rate * (update + weight_decay * weight), first_new, second_new)


def even_rows(weights, count, lead, base):
    halo = weights.shape[0] - base
    devices = lax.axis_size("dp") * lax.axis_size("seq")
    last = lax.dynamic_slice_in_dim(weights, count - halo, halo, 0).astype(bf16)
    before = lax.ppermute(last, OWNERS, [(i, i + 1) for i in range(devices - 1)])
    joined = jnp.concatenate([before.astype(f32), weights], axis=0)
    return lax.dynamic_slice_in_dim(joined, halo - lead, base, 0).astype(bf16)


def owned_rows(block, count, lead, slot):
    halo = slot - block.shape[0]
    devices = lax.axis_size("dp") * lax.axis_size("seq")
    after = lax.ppermute(block[:halo], OWNERS, [(i + 1, i) for i in range(devices - 1)])
    joined = jnp.concatenate([block, after, jnp.zeros_like(after)], axis=0).astype(f32)
    picked = lax.dynamic_slice_in_dim(joined, lead, slot, 0)
    return jnp.where(jnp.arange(slot)[:, None] < count, picked, 0.0)


def exchange(value, bit, devices):
    return lax.ppermute(value, OWNERS, [(i, i ^ (1 << bit)) for i in range(devices)])


def sum_all(value, devices):
    for bit in range(devices.bit_length() - 1):
        value = value + exchange(value, bit, devices)
    return value


def split_rows(left, mine, base):
    order = jnp.arange(D)
    within = order % (D // 2)
    lowest = jnp.where(order < D // 2, 1 - mine % 2, mine % 2)
    source = (2 * (within // base) + lowest) * base + within % base
    pick = (jnp.arange(D)[:, None] == source[None, :]).astype(bf16)
    return jnp.dot(left, pick, preferred_element_type=f32).astype(bf16)


def orders_of(devices, pieces):
    rest = list(range(3, devices.bit_length() - 1))
    return [[1, 2] + rest, [2, 1] + rest, rest[:2] + [1, 2] + rest[2:]][:pieces]


class Reduce:
    def __init__(self, left, right, mine, base, devices, cuts):
        bits = devices.bit_length() - 1
        self.mine, self.devices, self.step = mine, devices, 0
        self.orders = orders_of(devices, len(cuts) + 1)
        self.axes = [list(range(bits - 1, 0, -1)) for _ in self.orders]
        pieces = [right[:, begin:end] for begin, end in zip((0,) + cuts, cuts + (right.shape[1],))]

        def product(features, piece):
            return lax.dot_general(features, piece, (((0,), (0,)), ((), ())), preferred_element_type=f32)

        sent = [exchange(product(left[:, : D // 2], piece).astype(bf16), 0, devices) for piece in pieces]
        self.values = [
            (product(left[:, D // 2 :], piece) + got.astype(f32))
            .astype(bf16)
            .reshape([2] * (bits - 1) + [base, piece.shape[1]])
            for piece, got in zip(pieces, sent)
        ]

    def advance(self):
        for piece, (order, axes) in enumerate(zip(self.orders, self.axes)):
            bit, value = order[self.step], self.values[piece]
            axis, own = axes.index(bit), (self.mine >> bit) & 1
            sent = lax.dynamic_index_in_dim(value, 1 - own, axis, keepdims=False).astype(bf16)
            kept = lax.dynamic_index_in_dim(value, own, axis, keepdims=False).astype(f32)
            value = kept + exchange(sent, bit, self.devices).astype(f32)
            self.values[piece] = value.astype(bf16) if self.step == 0 else value
            axes.remove(bit)
        self.step += 1

    def result(self):
        while self.step < len(self.orders[0]):
            self.advance()
        return jnp.concatenate(self.values, axis=1)


def tie(value, *works):
    value, states = lax.optimization_barrier((value, [work.values for work in works]))
    for work, state in zip(works, states):
        work.values = state
    return value


def dot(a, b):
    return lax.dot_general(a, b, (((1,), (0,)), ((), ())), preferred_element_type=f32)


def dot_t(a, b):
    return lax.dot_general(a, b, (((1,), (1,)), ((), ())), preferred_element_type=f32)


def first_head(shape):
    return lax.broadcasted_iota(jnp.int32, shape, 1) < P_SIZE


def spread(columns, kind, left):
    return jnp.where(left, columns[:, kind : kind + 1], columns[:, 4 + kind : 5 + kind])


def note_heads(ref, value, first, left):
    lane = lax.broadcasted_iota(jnp.int32, ref.shape, 1) - first - 2 * pl.program_id(0)
    low = jnp.sum(jnp.where(left, value, 0.0), axis=1, keepdims=True)
    high = jnp.sum(jnp.where(left, 0.0, value), axis=1, keepdims=True)
    ref[...] += jnp.where(lane == 0, low, jnp.where(lane == 1, high, 0.0))


def sigmoid(v):
    return 1.0 / (1.0 + jnp.exp(-v))


def forward_kernel(
    x_ref, z_ref, cols_ref, rows_ref, g_ref, q_ref, state_ref, mask_ref, skip_ref, y_ref, gy_ref, ss_ref
):
    length = x_ref.shape[0]
    step = min(256, length)
    left = first_head(x_ref.shape)
    cols = cols_ref[0]
    x = x_ref[...].astype(f32) * mask_ref[...]
    xb = x.astype(bf16)
    inter = dot(q_ref[...], state_ref[...].astype(bf16)) * spread(cols, 3, left)
    parts = []
    for t in range(0, length, step):
        width = t + step
        outs = []
        for h in range(2):
            fall = jnp.minimum(cols[t:width, 4 * h : 4 * h + 1] - rows_ref[0, 2 * h : 2 * h + 1, :width], 0.0)
            mixing = g_ref[t:width, :width] * jnp.exp(fall) * rows_ref[0, 2 * h + 1 : 2 * h + 2, :width]
            outs.append(dot(mixing.astype(bf16), xb[:width]))
        parts.append(jnp.where(left[t:width], outs[0], outs[1]))
    y = jnp.concatenate(parts, axis=0) + inter + skip_ref[...] * x
    z = z_ref[...].astype(f32)
    gy = y * (z * sigmoid(z)) * mask_ref[...]
    y_ref[...] = y
    gy_ref[...] = gy

    @pl.when(pl.program_id(0) == 0)
    def _():
        ss_ref[...] = jnp.zeros_like(ss_ref)

    ss_ref[...] += gy * gy


def backward_kernel(
    do_ref, y_ref, z_ref, x_ref, cols_ref, rows_ref, gt_ref, state_ref, tok_ref, mask_ref, skip_ref,
    gain_ref, dx_ref, dgt_ref, dq_ref, heads_ref, vec_ref,
):
    length = x_ref.shape[0]
    step = min(256, length)
    left = first_head(x_ref.shape)
    cols = cols_ref[0]
    mask, skip, gain = mask_ref[...], skip_ref[...], gain_ref[...]
    r, pull = tok_ref[:, 0:1], tok_ref[:, 1:2]
    x = x_ref[...].astype(f32) * mask
    y = y_ref[...]
    z = z_ref[...].astype(f32)
    sig = sigmoid(z)
    gate = z * sig * mask
    gy = y * gate
    do = do_ref[...]
    dgy = r * do * gain - gy * pull
    dy = dgy * gate
    vec_ref[0:1, :] = jnp.sum(do * gy * r, axis=0, keepdims=True)
    vec_ref[1:2, :] = jnp.sum(dy * x, axis=0, keepdims=True)
    vec_ref[2:8, :] = jnp.zeros((6, 128), f32)
    dyb = dy.astype(bf16)
    entering = (dy * spread(cols, 3, left)).astype(bf16)
    stateb = state_ref[...].astype(bf16)

    @pl.when(pl.program_id(0) == 0)
    def _():
        dgt_ref[...] = jnp.zeros_like(dgt_ref)
        dq_ref[...] = jnp.zeros_like(dq_ref)
        heads_ref[...] = jnp.zeros_like(heads_ref)

    dq_ref[...] += dot_t(entering, stateb)
    xh = [jnp.where(left, x, 0.0).astype(bf16), jnp.where(left, 0.0, x).astype(bf16)]
    parts = []
    for s in range(0, length, step):
        outs = []
        total = None
        for h in range(2):
            here = cols[s : s + step]
            decay = jnp.exp(jnp.minimum(rows_ref[0, 2 * h : 2 * h + 1, s:] - here[:, 4 * h : 4 * h + 1], 0.0))
            outs.append(dot((gt_ref[s : s + step, s:] * decay).astype(bf16), dyb[s:]))
            part = dot_t(xh[h][s : s + step], dyb[s:]) * decay * here[:, 4 * h + 1 : 4 * h + 2]
            total = part if total is None else total + part
        dgt_ref[s : s + step, s:] += total
        parts.append(jnp.where(left[s : s + step], outs[0], outs[1]))
    u = jnp.concatenate(parts, axis=0)
    dx_ref[...] = spread(cols, 1, left) * u + skip * dy
    row = dy * (y - skip * x)
    xu = x * u
    note_heads(heads_ref, row, 0, left)
    note_heads(heads_ref, xu, H, left)


def conv_back(dact, in_ref, rim_ref, taps_ref, pad_ref, dc_ref, out_ref, vec_ref, edge_ref):
    length = in_ref.shape[0]
    pad_ref[0:8, :] = rim_ref[...].astype(f32)
    pad_ref[8 : 8 + length, :] = in_ref[...].astype(f32)
    c = taps_ref[4:5, :]
    for k in range(K):
        c = c + taps_ref[k : k + 1, :] * pad_ref[5 + k : 5 + k + length, :]
    sig = sigmoid(c)
    dc = dact * sig * (1.0 + c * (1.0 - sig))
    dc_ref[0:8, :] = jnp.zeros((8, 128), f32)
    dc_ref[8 : 8 + length, :] = dc
    dc_ref[8 + length : 16 + length, :] = jnp.zeros((8, 128), f32)
    for k in range(K):
        vec_ref[k : k + 1, :] = jnp.sum(dc * pad_ref[5 + k : 5 + k + length, :], axis=0, keepdims=True)
    vec_ref[4:5, :] = jnp.sum(dc, axis=0, keepdims=True)
    vec_ref[5:8, :] = jnp.zeros((3, 128), f32)
    grad = jnp.zeros((length + 8, 128), f32)
    for k in range(K):
        grad = grad + taps_ref[k : k + 1, :] * dc_ref[3 - k : 3 - k + length + 8, :]
    out_ref[...] = grad[8:].astype(bf16)
    edge_ref[0:8, :] = grad[:8]
    edge_ref[8:16, :] = grad[length:]


def inner_kernel(
    first, dx_ref, x_ref, cols_ref, k_ref, later_ref, mask_ref, in_ref, rim_ref, taps_ref, out_ref, vec_ref, edge_ref,
    heads_ref, dk_ref, pad_ref, dc_ref,
):
    left = first_head(x_ref.shape)
    cols = cols_ref[0]
    mask = mask_ref[...]
    x = x_ref[...].astype(f32) * mask
    later = later_ref[...].astype(bf16)
    tail, steps = spread(cols, 2, left), spread(cols, 1, left)
    u = dot(k_ref[...], later) * tail
    xu = x * u

    @pl.when(pl.program_id(0) == 0)
    def _():
        dk_ref[...] = jnp.zeros_like(dk_ref)
        heads_ref[...] = jnp.zeros_like(heads_ref)

    note_heads(heads_ref, xu, first, left)

    dk_ref[...] += dot_t((x * tail * steps).astype(bf16), later)
    dact = (dx_ref[...] + steps * u) * mask
    conv_back(dact, in_ref, rim_ref, taps_ref, pad_ref, dc_ref, out_ref, vec_ref, edge_ref)


def outer_kernel(dact_ref, in_ref, rim_ref, taps_ref, out_ref, vec_ref, edge_ref, pad_ref, dc_ref):
    conv_back(dact_ref[...], in_ref, rim_ref, taps_ref, pad_ref, dc_ref, out_ref, vec_ref, edge_ref)


def lanes(rows, shift=0):
    return pl.BlockSpec((rows, 128), lambda i: (0, i + shift))


def whole(rows, width):
    return pl.BlockSpec((rows, width), lambda i: (0, 0))


def planes(rows, width, shift=0):
    return pl.BlockSpec((1, rows, width), lambda i: (i + shift, 0, 0))


def run(kernel, steps, ins, outs, shapes, scratch=(), micros=2):
    return pl.pallas_call(
        kernel,
        grid=(steps,),
        in_specs=ins,
        out_specs=outs,
        out_shape=[jax.ShapeDtypeStruct(*shape) for shape in shapes],
        scratch_shapes=list(scratch),
        compiler_params=pltpu.CompilerParams(vmem_limit_bytes=48 * 1024 * 1024),
        cost_estimate=pl.CostEstimate(flops=micros * 10**9, transcendentals=0, bytes_accessed=micros * 3 * 10**6),
    )


def hand_on(fresh, carry, backward):
    count = lax.axis_size("seq")
    entered = jnp.zeros_like(fresh)
    for i in range(count - 1):
        leaving = (fresh + carry * entered).astype(bf16)
        route = [(count - 1 - i, count - 2 - i)] if backward else [(i, i + 1)]
        entered = entered + lax.ppermute(leaving, "seq", route).astype(f32)
    return entered


def local(
    hidden,
    grad_out,
    doc_lengths,
    resets,
    width_index,
    owner_counts,
    w_in,
    m_in,
    v_in,
    w_out,
    m_out,
    v_out,
    small_params,
    small_m,
    small_v,
):
    T = hidden.shape[0]
    slot = w_in.shape[0]
    seq_count = lax.axis_size("seq")
    devices = lax.axis_size("dp") * seq_count
    base = D // devices
    mine = lax.axis_index("dp") * seq_count + lax.axis_index("seq")
    gain_in, conv_weight, conv_bias, dt_bias, decay_log, skip_gain, gain_out = unpack(small_params)
    channel_mask, active = width_mask(width_index[0])
    before = jnp.arange(devices) < mine
    lead = jnp.sum(jnp.where(before, owner_counts, 0)) * RB - mine * base
    count = owner_counts[mine] * RB

    even_in = even_rows(w_in, count, lead, base)
    even_out = even_rows(w_out, count, lead, base)
    weights_x = lax.all_gather(even_in[:, E:], OWNERS, axis=0, tiled=True)
    weights_z = lax.all_gather(even_in[:, :E], OWNERS, axis=0, tiled=True)
    hidden_full = hidden.astype(f32)
    scale = lax.rsqrt(jnp.mean(hidden_full * hidden_full, axis=1, keepdims=True) + norm_eps)
    normed = (hidden_full * scale * gain_in[None, :]).astype(bf16)
    tokens_out, features = split_rows(grad_out, mine, base), split_rows(normed, mine, base)
    weights_x, tokens_out, features = lax.optimization_barrier((weights_x, tokens_out, features))
    proj_x = jnp.dot(normed, weights_x, preferred_element_type=f32).astype(bf16)
    conv_in = proj_x[:, :CW]
    raw = proj_x[:, CW:].astype(f32) + dt_bias[None, :]
    route = [(i, i + 1) for i in range(seq_count - 1)]
    rim = lax.ppermute(conv_in[T - (K - 1) :], "seq", route)
    padded = jnp.concatenate([rim, conv_in], axis=0).astype(f32)
    mixed = conv_bias[None, :] + sum(
        (conv_weight[tap][None, :] * padded[tap : tap + T] for tap in range(K))
    )
    act = (mixed * sigmoid(mixed)).astype(bf16)
    keys, queries = act[:, E : E + N], act[:, E + N :]

    positions = lax.axis_index("seq") * T + jnp.arange(T)
    flags = reset_flags(doc_lengths[0], resets[0], positions)
    steps = jax.nn.softplus(raw)
    rate = jnp.exp(decay_log)[None, :]
    order = jnp.arange(T)
    lower = (order[:, None] >= order[None, :]).astype(f32)
    sums = jnp.dot(
        lower,
        jnp.concatenate([-rate * steps, jnp.broadcast_to(flags[:, None], (T, H))], axis=1),
        precision=lax.Precision.HIGHEST,
    )
    total, segment = sums[:, :H], jnp.round(sums[:, H])
    enter = jnp.exp(total) * (segment == 0)[:, None]
    tail = jnp.exp(total[-1:] - total) * (segment == segment[-1])[:, None]
    carry = jnp.repeat(enter[-1], P_SIZE)[None, :]
    cols = jnp.stack([total, steps, tail, enter], axis=2).reshape(T, PAIRS, 8).transpose(1, 0, 2)
    rows = jnp.stack([total.T, steps.T], axis=1).reshape(PAIRS, 4, T)
    allowed = (segment[:, None] == segment[None, :]) & (order[:, None] >= order[None, :])
    scores = jnp.where(allowed, jnp.einsum("tn,sn->ts", queries, keys, preferred_element_type=f32), 0.0)
    mask_row, skip_row = channel_mask[None, :], jnp.repeat(skip_gain, P_SIZE)[None, :]
    gain_row = gain_out[None, :]

    heads_of = (jnp.arange(E)[None, :] // P_SIZE == jnp.arange(H)[:, None]).astype(bf16)
    weight = jnp.dot((tail * steps).astype(bf16), heads_of, preferred_element_type=f32)
    handed = (act[:, :E].astype(f32) * mask_row * weight).astype(bf16)
    fresh = jnp.dot(keys.T, handed, preferred_element_type=f32)
    entry = jnp.dot(enter.astype(bf16), heads_of, preferred_element_type=f32).astype(bf16)
    even_out, weights_z, fresh, cols, rows, scores, entry = lax.optimization_barrier(
        (even_out, weights_z, fresh, cols, rows, scores, entry)
    )
    weights_out = lax.all_gather(even_out, OWNERS, axis=0, tiled=True)
    entered = hand_on(fresh, carry, False)
    gate_raw = jnp.dot(normed, weights_z, preferred_element_type=f32).astype(bf16)
    y, gated, squares = run(
        forward_kernel,
        PAIRS,
        [lanes(T), lanes(T), planes(T, 8), planes(4, T), whole(T, T), whole(T, N), lanes(N), lanes(1), lanes(1)],
        [lanes(T), lanes(T), whole(T, 128)],
        [((T, E), f32), ((T, E), f32), ((T, 128), f32)],
        micros=34,
    )(act, gate_raw, cols, rows, scores, queries, entered, mask_row, skip_row)
    root = lax.rsqrt(jnp.sum(squares, axis=1, keepdims=True) / active + norm_eps)
    mixed_low = (gated * root * gain_row).astype(bf16)
    out = Reduce(tokens_out, mixed_low, mine, base, devices, (2048,))
    weights_out = tie(weights_out, out)
    out.advance()
    mixed_grad = jnp.dot(grad_out, weights_out, preferred_element_type=f32)
    pull = root**3 * jnp.sum(mixed_grad * gain_row * gated, axis=1, keepdims=True) / active
    gate_full = gate_raw.astype(f32)
    open_part = sigmoid(gate_full)
    grad_gated = root * mixed_grad * gain_row - gated * pull
    grad_gate = grad_gated * y * mask_row * open_part * (1.0 + gate_full * (1.0 - open_part))
    grad_gate = grad_gate.astype(bf16)
    entering = (grad_gated * (gate_full * open_part) * mask_row * entry).astype(bf16)
    grad_entered = jnp.dot(queries.T, entering, preferred_element_type=f32)
    work_z = Reduce(features, grad_gate, mine, base, devices, (2048,))
    mixed_grad = tie(mixed_grad, out, work_z)
    out.advance()
    work_z.advance()
    tok = jnp.concatenate([root, pull, jnp.zeros((T, 6), f32)], axis=1)
    grad_x, grad_scores, grad_queries, heads_a, vec_a = run(
        backward_kernel,
        PAIRS,
        [
            lanes(T), lanes(T), lanes(T), lanes(T), planes(T, 8), planes(4, T), whole(T, T), lanes(N), whole(T, 8),
            lanes(1), lanes(1), lanes(1),
        ],
        [lanes(T), whole(T, T), whole(T, N), whole(T, 128), lanes(8)],
        [((T, E), f32), ((T, T), f32), ((T, N), f32), ((T, 128), f32), ((8, E), f32)],
        micros=45,
    )(mixed_grad, y, gate_raw, act, cols, rows, scores.T, entered, tok, mask_row, skip_row, gain_row)
    later = hand_on(grad_entered, carry, True)
    grad_x, grad_gate = tie((grad_x, grad_gate), out, work_z)
    out.advance()
    work_z.advance()
    du = jnp.einsum("tc,dc->td", grad_gate, weights_z, preferred_element_type=f32)
    later, du = tie((later, du), out, work_z)
    out.advance()
    work_z.advance()
    rim8 = jnp.concatenate([jnp.zeros((8 - (K - 1), CW), bf16), rim], axis=0)
    taps = jnp.concatenate([conv_weight, conv_bias[None, :], jnp.zeros((3, CW), f32)], axis=0)
    scratch = (pltpu.VMEM((T + 16, 128), f32), pltpu.VMEM((T + 16, 128), f32))
    part = PAIRS // 2

    def inner_half(shift, later):
        return run(
            partial(inner_kernel, 2 * shift),
            part,
            [
                lanes(T, shift), lanes(T, shift), planes(T, 8, shift), whole(T, N), lanes(N, shift), lanes(1, shift),
                lanes(T, shift), lanes(8, shift), lanes(8, shift),
            ],
            [lanes(T), lanes(8), lanes(16), whole(T, 128), whole(T, N)],
            [((T, E // 2), bf16), ((8, E // 2), f32), ((16, E // 2), f32), ((T, 128), f32), ((T, N), f32)],
            scratch,
            micros=18,
        )(grad_x, act, cols, keys, later, mask_row, proj_x, rim8, taps)

    def ends_of(edges):
        route = [(i + 1, i) for i in range(seq_count - 1)]
        pushed = lax.ppermute(edges[8 - (K - 1) : 8], "seq", route)
        kept = jnp.zeros((8 - (K - 1), edges.shape[1]), f32)
        return (edges[8:] + jnp.concatenate([kept, pushed], axis=0)).astype(bf16)

    inner_a, vec_a2, edge_a, heads_b, keys_a = inner_half(0, later)
    grad_proj_a = lax.dynamic_update_slice(inner_a, ends_of(edge_a), (T - 8, 0))
    work_a = Reduce(features, grad_proj_a, mine, base, devices, (1024,))
    later_b = tie(later, out, work_z, work_a)
    work_a.advance()
    inner_b, vec_b, edge_b, heads_c, grad_keys = inner_half(part, later_b)
    inner_b, grad_keys = tie((inner_b, grad_keys), work_a)
    work_z.advance()
    work_a.advance()
    grad_keys = grad_keys + keys_a
    pairs_t = jnp.where(allowed.T, grad_scores, 0.0).astype(bf16)
    grad_keys = grad_keys + jnp.dot(pairs_t, queries, preferred_element_type=f32)
    grad_queries = grad_queries + jnp.einsum("st,sn->tn", pairs_t, keys, preferred_element_type=f32)
    outer, vec_c, edge_c = run(
        outer_kernel,
        2,
        [lanes(T), lanes(T, PAIRS), lanes(8, PAIRS), lanes(8, PAIRS)],
        [lanes(T), lanes(8), lanes(16)],
        [((T, 2 * N), bf16), ((8, 2 * N), f32), ((16, 2 * N), f32)],
        scratch,
    )(jnp.concatenate([grad_keys, grad_queries], axis=1), proj_x, rim8, taps)
    ends = ends_of(jnp.concatenate([edge_b, edge_c], axis=1))

    along = heads_a[:, H:] + heads_b[:, :H] + heads_c[:, :H]
    leaving = carry * entered + fresh
    crossing = jnp.sum((later * leaving).reshape(N, H, P_SIZE), axis=(0, 2))
    upper = (order[:, None] <= order[None, :]).astype(f32)
    grad_logs = crossing[None, :] + jnp.dot(
        upper, heads_a[:, :H] - steps * along, precision=lax.Precision.HIGHEST
    )
    grad_raw = (along - rate * grad_logs) * jax.nn.sigmoid(raw)
    conv_vec = jnp.concatenate([vec_a2, vec_b, vec_c], axis=1)
    grad_proj = jnp.concatenate([inner_b, outer, grad_raw.astype(bf16)], axis=1)
    grad_proj = lax.dynamic_update_slice(grad_proj, ends, (T - 8, 0))
    grad_proj = tie(grad_proj, work_a, work_z)
    work_a.advance()
    work_x = Reduce(features, grad_proj, mine, base, devices, (1024, 2048))

    grad_last, last_low = tie((grad_proj, mixed_low), work_x, work_a)
    work_x.advance()
    work_a.advance()
    du = du + jnp.einsum("tc,dc->td", grad_proj_a, weights_x[:, : E // 2], preferred_element_type=f32)
    du = du + jnp.einsum("tc,dc->td", grad_last, weights_x[:, E // 2 :], preferred_element_type=f32)
    branch = jnp.einsum("te,de->td", last_low, weights_out, preferred_element_type=f32)
    output = (hidden_full + branch).astype(bf16)
    dug = du * gain_in[None, :]
    inward = jnp.mean(dug * hidden_full, axis=1, keepdims=True)
    input_grad = grad_out.astype(f32) + scale * dug - hidden_full * scale**3 * inward
    small_grad = jnp.concatenate(
        [
            jnp.sum(du * hidden_full * scale, axis=0),
            conv_vec[:K].reshape(-1),
            conv_vec[K],
            jnp.sum(grad_raw, axis=0),
            -rate[0] * jnp.sum(steps * grad_logs, axis=0),
            jnp.sum(vec_a[1].reshape(H, P_SIZE), axis=1),
            vec_a[0],
        ]
    )

    output, input_grad = tie((output, input_grad), work_x, work_a)

    block_out, block_z = out.result(), work_z.result()
    block_x = jnp.concatenate([work_a.result(), work_x.result()], axis=1)
    block_in = jnp.concatenate([block_z, block_x], axis=1)
    big_square = jnp.sum(block_in**2) + jnp.sum(block_out**2)
    packed = jnp.concatenate([small_grad, jnp.full((64,), big_square)]).reshape(-1, 128)
    packed = sum_all(packed, devices).reshape(-1)
    small_total, square_total = packed[: small_grad.shape[0]], packed[small_grad.shape[0]]
    owned_in = owned_rows(block_in, count, lead, slot)
    owned_out = owned_rows(block_out, count, lead, slot)
    norm = jnp.sqrt(square_total + jnp.sum(small_total * small_total))
    clip = 1.0 / jnp.maximum(norm, 1.0)
    correction = jnp.float32(bias_fix)
    w_in_new, m_in_new, v_in_new = adamw(w_in, m_in, v_in, owned_in * clip, rate_matrix, correction)
    w_out_new, m_out_new, v_out_new = adamw(
        w_out, m_out, v_out, owned_out * clip, rate_matrix, correction
    )
    small_new, small_m_new, small_v_new = adamw(
        small_params, small_m, small_v, small_total * clip, rate_vector, correction
    )
    return (
        output,
        input_grad,
        w_in_new,
        m_in_new,
        v_in_new,
        w_out_new,
        m_out_new,
        v_out_new,
        small_new,
        small_m_new,
        small_v_new,
        owned_in,
        owned_out,
        small_total,
        norm.reshape(1),
    )


def solution(mesh):
    tokens, row, whole_array = P(OWNERS, None), P("dp", None), P()
    in_specs = (tokens, tokens, row, row, P("dp"), whole_array) + (tokens,) * 6 + (whole_array,) * 3
    out_specs = (tokens,) * 8 + (whole_array,) * 3 + (tokens,) * 2 + (whole_array,) * 2
    return jax.shard_map(local, mesh=mesh, in_specs=in_specs, out_specs=out_specs, check_vma=False)
```
